128 devices in a mesh: sub: 64 (over z, y, x), front: 2 (over core).
Axes of the slice: x: 4, y: 4, z: 4, core: 2. Of those that a mesh axis runs over, the one named last changes fastest.
Arguments:
- piv_cols: bfloat16 [64, 3072, 1024], P('sub', None, 'front'), may hold values from -6 to 6
- trail_cols: bfloat16 [64, 3072, 2048], P('sub', None, 'front'), may hold values from -6 to 6
- row_end: int32 [64, 24], P('sub'), may hold values from 128 to 3072, as said below
- parent_of: int32 [64], P('sub'), may hold values from 0 to 1, as said below
Outputs:
- r_pivot: float32 [2, 1024, 1024], P(None, None, 'front')
- r_trail: float32 [2, 1024, 2048], P(None, None, 'front')
The draws below stay inside these ranges and needn't reach their ends.
Inputs may be any that keep to these rules, and one draw needn't show every extreme that they name: row_end[c, j] is a multiple of 128 and never falls as j grows; in the column blocks j < 8 it is at most 1280, and it reaches 1280 for some child in every draw. `parent_of`: exactly 32 children have each parent.
All inputs are finite; a program needn't handle non-finite values.
Results may differ from the reference program's by a relative error of at most 0.0003.
Values may be sent and summed in bfloat16 or wider, within the bound.
A program may use at most 128 MiB of HBM per device.

```python
import jax
import jax.numpy as jnp
from jax import lax

W = 3072
BLK = 128
KROWS = 3072
NPAR = 2
KIDS = 64
PIV = 1024
NB = 24


def draw_row_end(key, part):
    jumps = jax.random.randint(key, (KIDS, NB), 0, 3)
    chosen = jax.random.randint(jax.random.fold_in(key, 7), (), 0, KIDS)
    columns = jnp.arange(NB, dtype=jnp.int32)
    force = (jnp.arange(KIDS, dtype=jnp.int32)[:, None] == chosen) & (columns[None, :] == PIV // BLK - 1)
    jumps = jnp.where(force, 2, jumps)
    reach = lax.cummax(columns[None, :] + 1 + jumps, axis=1)
    return (BLK * jnp.minimum(reach, KROWS // BLK)).astype(jnp.int32)


def draw_parent_of(key, part):
    return (jax.random.permutation(key, KIDS) % NPAR).astype(jnp.int32)


def block_scale(own_key, extent, split, smallest, largest):
    level, own = 1.0, jax.random.fold_in(own_key, 6)
    for dim, parts in split:
        steps = jnp.exp(jax.random.uniform(jax.random.fold_in(own, dim), (parts,), jnp.float32, smallest / len(split), largest / len(split)))
        level = level * jnp.repeat(steps, extent[dim] // parts).reshape([-1 if axis == dim else 1 for axis in range(len(extent))])
    return level


def normal_values(key, shape, deviation, bound, pieces=(), kind=jnp.bfloat16):
    loudness = block_scale(key, shape, pieces, -0.22, 0.18) if pieces else 1.0
    array = jax.random.normal(key, shape, jnp.float32) * deviation * loudness
    return jnp.minimum(jnp.maximum(array, -bound), bound).astype(kind)


def setup_inputs(seed: int = 0) -> dict:
    keys = jax.random.split(jax.random.key(seed), 5)
    return {
        "piv_cols": normal_values(keys[0], (KIDS, KROWS, PIV), 1.0, 6.0, ((0, 64), (2, 2))),
        "trail_cols": normal_values(keys[1], (KIDS, KROWS, W - PIV), 1.0, 6.0, ((0, 64), (2, 2))),
        "row_end": draw_row_end(jax.random.fold_in(keys[4], 71), 0),
        "parent_of": draw_parent_of(jax.random.fold_in(keys[4], 71), 0),
    }


def reference(piv_cols, trail_cols, row_end, parent_of):
    row_ids = jnp.arange(KROWS, dtype=jnp.int32)[:, None]
    piv_block = (jnp.arange(PIV, dtype=jnp.int32) // BLK).astype(jnp.int32)
    trail_block = ((PIV + jnp.arange(W - PIV, dtype=jnp.int32)) // BLK).astype(jnp.int32)
    parent_ids = jnp.arange(NPAR, dtype=jnp.int32)

    def add_child(total, item):
        pivot, trail, stair_ends, parent = item
        live_pivot = row_ids < stair_ends[piv_block][None, :]
        live_trail = row_ids < stair_ends[trail_block][None, :]
        pivot = jnp.where(live_pivot, pivot, jnp.zeros((), pivot.dtype))
        trail = jnp.where(live_trail, trail, jnp.zeros((), trail.dtype))
        whole = jnp.concatenate([pivot, trail], axis=1)
        gram = jnp.dot(pivot.T.astype(jnp.float32), whole.astype(jnp.float32), preferred_element_type=jnp.float32)
        parent_pick = (parent_ids == parent).astype(jnp.float32)
        return (total + parent_pick[:, None, None] * gram[None], None)
    start = jnp.zeros((NPAR, PIV, W), jnp.float32)
    total, _ = lax.scan(add_child, start, (piv_cols, trail_cols, row_end, parent_of))
    factor_lower = jnp.linalg.cholesky(total[:, :, :PIV])
    r_pivot = jnp.transpose(factor_lower, (0, 2, 1))
    r_trail = lax.linalg.triangular_solve(factor_lower, total[:, :, PIV:], left_side=True, lower=True)
    return (r_pivot, r_trail)
```

```python
import jax
import jax.numpy as jnp
from jax import lax
from jax.experimental import pallas as pl
from jax.experimental.pallas import tpu as pltpu
from jax.sharding import PartitionSpec as P

F32 = jnp.float32
HI = lax.Precision.HIGHEST
MESH = pl.DeviceIdType.MESH
LIVE = 1280
N = 1024
T = 1024
COLORS = 6
CW = 256
STEPS = 6


def dims_of(sub):
    x, y, z = sub % 4, (sub // 4) % 4, sub // 16
    partner, side = [], []
    for kind in range(2):
        for coord, stride in ((x, 1), (y, 4), (z, 16)):
            if kind == 0:
                other, bit = coord + 1 - 2 * (coord % 2), ((coord + 1) // 2) % 2
            else:
                other, bit = 3 - coord, coord // 2
            partner.append(sub + (other - coord) * stride)
            side.append(bit)
    return partner, side


def reduce_kernel(piv, trail, row_end, parent, out, out_pair, half_in, cols_in, g, work, total, pair,
                  r0, r1, r2, r3, r4, r5, pids, in_sem, send, recv, psend, precv, dsend, drecv, hsend, hrecv, out_sem):
    front = lax.axis_index("front")
    sub = lax.axis_index("sub")
    partner, side = dims_of(sub)
    inbox = (r0, r1, r2, r3, r4, r5)

    local = [
        pltpu.make_async_copy(piv.at[0, pl.ds(0, LIVE), :], half_in.at[front], in_sem.at[0])
    ]
    for q in range(COLORS):
        src = piv if q < 2 else trail
        c = CW * (q if q < 2 else q - 2)
        local.append(pltpu.make_async_copy(src.at[0, pl.ds(0, LIVE), pl.ds(c, CW)], cols_in.at[q], in_sem.at[1 + q]))
    for copy in local:
        copy.start()

    barrier = pltpu.get_barrier_semaphore()
    for d in range(6):
        pl.semaphore_signal(barrier, inc=1, device_id={"sub": partner[d]}, device_id_type=MESH)
    pl.semaphore_signal(barrier, inc=1, device_id={"front": 1 - front}, device_id_type=MESH)
    pl.semaphore_wait(barrier, 7)

    half = pltpu.make_async_remote_copy(
        piv.at[0, pl.ds(0, LIVE), :], half_in.at[front], hsend, hrecv,
        device_id={"front": 1 - front}, device_id_type=MESH)
    half.start()
    pid_copies = []
    for q in range(COLORS):
        copy = pltpu.make_async_remote_copy(
            parent, pids.at[q], psend.at[q], precv.at[q],
            device_id={"sub": partner[q]}, device_id_type=MESH)
        copy.start()
        pid_copies.append(copy)

    row_ids = lax.broadcasted_iota(jnp.int32, (LIVE, 512), 0)
    block_ids = lax.broadcasted_iota(jnp.int32, (LIVE, 512), 1) // 128

    def masked(which):
        ends = jnp.zeros((LIVE, 512), jnp.int32)
        for b in range(4):
            ends = jnp.where(block_ids == b, row_end[0, which * 4 + b], ends)
        value = half_in[which].astype(F32)
        return jnp.where(row_ids < ends, value, 0.0).astype(jnp.bfloat16)

    def product(which, q):
        rows = pl.ds(pl.multiple_of(which * 512, 512), 512)
        g[q, rows, :] = lax.dot_general(
            half_in[which], cols_in[q], (((0,), (0,)), ((), ())), preferred_element_type=F32)

    for copy in local:
        copy.wait()
    half_in[front] = masked(front)

    @pl.loop(0, COLORS)
    def _(q):
        product(front, q)

    half.wait()
    half_in[1 - front] = masked(1 - front)

    off = [0] * COLORS
    rel = [0] * COLORS
    scatter = {}

    def start_scatter(q, s):
        d = (q + s) % 6
        h = 512 >> s
        away = pl.ds(pl.multiple_of((rel[q] if s else 0) + (1 - side[d]) * h, 8), h)
        src = work.at[q, :, away, :] if s else g.at[q, away, :]
        copy = pltpu.make_async_remote_copy(
            src, inbox[s].at[q], send.at[q, s], recv.at[q, s],
            device_id={"sub": partner[d]}, device_id_type=MESH)
        copy.start()
        scatter[q, s] = copy

    for q in range(COLORS):
        product(1 - front, q)
        start_scatter(q, 0)

    for s in range(STEPS):
        for q in range(COLORS):
            d = (q + s) % 6
            h = 512 >> s
            off[q] = off[q] + side[d] * h
            if s:
                rel[q] = rel[q] + side[d] * h
            step = min(h, 64)
            base = rel[q] if s else off[q]
            scatter[q, s].wait()
            if s == 0:
                pid_copies[q].wait()
                own, other = parent[0:1, 0:1], pids[q, 0:1, 0:1]
                weights = [((own == p).astype(F32), (other == p).astype(F32)) for p in range(2)]

                @pl.loop(0, h // step)
                def _(i):
                    here = pl.ds(pl.multiple_of(base + i * step, 8), step)
                    there = pl.ds(pl.multiple_of(i * step, 8), step)
                    mine, theirs = g[q, here, :], inbox[0][q, there, :]
                    for p in range(2):
                        work[q, p, there, :] = mine * weights[p][0] + theirs * weights[p][1]
            elif s < STEPS - 1:
                @pl.loop(0, h // step)
                def _(i):
                    here = pl.ds(pl.multiple_of(base + i * step, 8), step)
                    there = pl.ds(pl.multiple_of(i * step, 8), step)
                    work[q, :, here, :] = work[q, :, here, :] + inbox[s][q, :, there, :]
            else:
                here = pl.ds(pl.multiple_of(base, 8), h)
                total[q, :, pl.ds(pl.multiple_of(off[q], 8), h), :] = work[q, :, here, :] + inbox[s][q]
            if s + 1 < STEPS:
                start_scatter(q, s + 1)

    gather, to_pair, outs = {}, {}, []

    def start_pair(q, k, start, size):
        if q >= 2:
            return
        rows = pl.ds(pl.multiple_of(start, 8), size)
        copy = pltpu.make_async_remote_copy(
            total.at[q, :, rows, :], pair.at[q, :, rows, :], dsend.at[q, k], drecv.at[q, k],
            device_id={"front": 1 - front}, device_id_type=MESH)
        copy.start()
        to_pair[q, k] = copy

    def start_gather(q, s):
        d = (q + s) % 6
        h = 512 >> s
        rows = pl.ds(pl.multiple_of(off[q], 8), h)
        copy = pltpu.make_async_remote_copy(
            total.at[q, :, rows, :], total.at[q, :, rows, :], send.at[q, 6 + s], recv.at[q, 6 + s],
            device_id={"sub": partner[d]}, device_id_type=MESH)
        copy.start()
        gather[q, s] = copy

    def start_out(q, k, start):
        rows = pl.ds(pl.multiple_of(start, 8), 512)
        copy = pltpu.make_async_copy(total.at[q, :, rows, :], out.at[q, :, rows, :], out_sem.at[q, k])
        copy.start()
        outs.append(copy)

    for q in range(COLORS):
        start_gather(q, 5)
        start_pair(q, 6, off[q], 16)
    for s in range(STEPS - 1, -1, -1):
        for q in range(COLORS):
            d = (q + s) % 6
            h = 512 >> s
            gather[q, s].wait()
            theirs = off[q] + (1 - 2 * side[d]) * h
            off[q] = off[q] - side[d] * h
            if s > 0:
                start_gather(q, s - 1)
            start_pair(q, s, theirs, h)
            if s == 1:
                start_out(q, 0, off[q])
            if s == 0:
                start_out(q, 1, theirs)
    for q in range(2):
        for k in range(7):
            to_pair[q, k].wait()
        copy = pltpu.make_async_copy(pair.at[q], out_pair.at[q], out_sem.at[q, 2])
        copy.start()
        outs.append(copy)
    for copy in outs:
        copy.wait()


def reduce_gram(piv, trail, row_end, parent):
    inbox = [pltpu.VMEM((COLORS, 512, CW), F32)]
    inbox += [pltpu.VMEM((COLORS, 2, 512 >> s, CW), F32) for s in range(1, STEPS)]
    dma = pltpu.SemaphoreType.DMA
    return pl.pallas_call(
        reduce_kernel,
        out_shape=(jax.ShapeDtypeStruct((COLORS, 2, N, CW), F32), jax.ShapeDtypeStruct((2, 2, N, CW), F32)),
        in_specs=[
            pl.BlockSpec(memory_space=pl.ANY),
            pl.BlockSpec(memory_space=pl.ANY),
            pl.BlockSpec(memory_space=pltpu.SMEM),
            pl.BlockSpec(memory_space=pltpu.VMEM),
        ],
        out_specs=[pl.BlockSpec(memory_space=pl.ANY)] * 2,
        scratch_shapes=[
            pltpu.VMEM((2, LIVE, 512), jnp.bfloat16),
            pltpu.VMEM((COLORS, LIVE, CW), jnp.bfloat16),
            pltpu.VMEM((COLORS, N, CW), F32),
            pltpu.VMEM((COLORS, 2, 512, CW), F32),
            pltpu.VMEM((COLORS, 2, N, CW), F32),
            pltpu.VMEM((2, 2, N, CW), F32),
            *inbox,
            pltpu.VMEM((COLORS, 8, 128), jnp.int32),
            dma((7,)),
            dma((COLORS, 12)),
            dma((COLORS, 12)),
            dma((COLORS,)),
            dma((COLORS,)),
            dma((2, 7)),
            dma((2, 7)),
            dma,
            dma,
            dma((COLORS, 3)),
        ],
        compiler_params=pltpu.CompilerParams(
            collective_id=0, has_side_effects=True, vmem_limit_bytes=60 * 2**20),
    )(piv, trail, row_end, parent)


def dot_n(a, b):
    return lax.dot_general(a, b, (((1,), (0,)), ((), ())), precision=HI, preferred_element_type=F32)


def dot_t(a, b):
    return lax.dot_general(a, b, (((0,), (0,)), ((), ())), precision=HI, preferred_element_type=F32)


def spread(x):
    return jnp.broadcast_to(x, (8, 128))


def leaf(s):
    sub = lax.broadcasted_iota(jnp.int32, (8, 256), 0)
    for g in range(16):
        for p in range(2):
            rows = [s[p, pl.ds(8 * g + j, 8, stride=0), :] for j in range(8)]
            if g < 15:
                nxt = s[p, 8 * g + 8 : 8 * g + 16, :]
                cols = [spread(nxt[:, 8 * g + j : 8 * g + j + 1]) for j in range(8)]
            a = {(i, j): spread(rows[i][:, 8 * g + j : 8 * g + j + 1]) for i in range(8) for j in range(i, 8)}
            m, u = {}, {}
            for k in range(8):
                r = lax.rsqrt(a[k, k])
                for j in range(k + 1, 8):
                    u[k, j] = a[k, j] * r
                m[k, k] = r
                for c in range(k):
                    m[k, c] = m[k, c] * r
                for i in range(k + 1, 8):
                    for j in range(i, 8):
                        a[i, j] = a[i, j] - u[k, i] * u[k, j]
                    for c in range(k + 1):
                        t = u[k, i] * m[k, c]
                        m[i, c] = (m[i, c] - t) if (i, c) in m else -t
            done = []
            for k in range(8):
                lo = sum(m[k, j] * rows[j][:, :128] for j in range(k + 1))
                hi = sum(m[k, j] * rows[j][:, 128:] for j in range(k + 1))
                done.append(jnp.concatenate([lo, hi], axis=1))
            out = done[0]
            for k in range(1, 8):
                out = jnp.where(sub == k, done[k], out)
            s[p, 8 * g : 8 * g + 8, :] = out
            if g < 15:
                lo, hi = nxt[:, :128], nxt[:, 128:]
                for k in range(8):
                    l = sum(m[k, j] * cols[j] for j in range(k + 1))
                    lo = lo - l * done[k][:, :128]
                    hi = hi - l * done[k][:, 128:]
                s[p, 8 * g + 8 : 8 * g + 16, :] = jnp.concatenate([lo, hi], axis=1)
            if g < 14:
                upd = dot_t(out[:, :128], out)
                s[p, 8 * g + 16 :, :] = s[p, 8 * g + 16 :, :] - upd[8 * g + 16 :, :]


def factor_kernel(gram, pair, r_pivot, r_trail, u, s, in_sem, out_sem):
    front = lax.axis_index("front")
    first = []
    second = []
    for p in range(2):
        for q in range(2):
            own = pl.ds(pl.multiple_of(front * 512 + q * CW, CW), CW)
            other = pl.ds(pl.multiple_of((1 - front) * 512 + q * CW, CW), CW)
            first.append(pltpu.make_async_copy(gram.at[q, p], u.at[p, :, own], in_sem.at[p, q]))
            first.append(pltpu.make_async_copy(pair.at[q, p], u.at[p, :, other], in_sem.at[p, 2 + q]))
        for q in range(2, COLORS):
            cols = pl.ds(N + (q - 2) * CW, CW)
            second.append(pltpu.make_async_copy(gram.at[q, p], u.at[p, :, cols], in_sem.at[p, 2 + q]))
    for copy in first + second:
        copy.start()
    for copy in first:
        copy.wait()
    ri = lax.broadcasted_iota(jnp.int32, (128, 128), 0)
    ci = lax.broadcasted_iota(jnp.int32, (128, 128), 1)

    def block(i):
        return pl.ds(pl.multiple_of(i * 128, 128), 128)

    @pl.loop(0, 8)
    def _(k):
        rs = block(k)
        for p in range(2):
            d = u[p, rs, rs]
            s[p, :, :128] = jnp.where(ri <= ci, d, jnp.transpose(d))
            s[p, :, 128:] = (ri == ci).astype(F32)
        leaf(s)

        @pl.when(k == 0)
        def _():
            for copy in second:
                copy.wait()

        for p in range(2):
            w = s[p, :, 128:]
            u[p, rs, rs] = jnp.where(ri <= ci, s[p, :, :128], 0.0)

            @pl.loop(0, k)
            def _(j):
                u[p, rs, block(j)] = jnp.zeros((128, 128), F32)

            @pl.loop(k + 1, 8)
            def _(j):
                u[p, rs, block(j)] = dot_n(w, u[p, rs, block(j)])

            u[p, rs, pl.ds(N, T)] = dot_n(w, u[p, rs, pl.ds(N, T)])

            @pl.loop(k + 1, 8)
            def _(i):
                l = jnp.transpose(u[p, rs, block(i)])

                @pl.loop(i, 8)
                def _(j):
                    u[p, block(i), block(j)] = u[p, block(i), block(j)] - dot_n(l, u[p, rs, block(j)])

                u[p, block(i), pl.ds(N, T)] = u[p, block(i), pl.ds(N, T)] - dot_n(l, u[p, rs, pl.ds(N, T)])

    outs = []
    for p in range(2):
        own = pl.ds(pl.multiple_of(front * 512, 512), 512)
        outs.append(pltpu.make_async_copy(u.at[p, :, own], r_pivot.at[p], out_sem.at[p, 0]))
        outs.append(pltpu.make_async_copy(u.at[p, :, pl.ds(N, T)], r_trail.at[p], out_sem.at[p, 1]))
    for copy in outs:
        copy.start()
    for copy in outs:
        copy.wait()


def factor(gram, pair):
    return pl.pallas_call(
        factor_kernel,
        out_shape=(jax.ShapeDtypeStruct((2, N, 512), F32), jax.ShapeDtypeStruct((2, N, T), F32)),
        in_specs=[pl.BlockSpec(memory_space=pl.ANY)] * 2,
        out_specs=[pl.BlockSpec(memory_space=pl.ANY)] * 2,
        scratch_shapes=[
            pltpu.VMEM((2, N, N + T), F32),
            pltpu.VMEM((2, 128, 256), F32),
            pltpu.SemaphoreType.DMA((2, 8)),
            pltpu.SemaphoreType.DMA((2, 2)),
        ],
        compiler_params=pltpu.CompilerParams(vmem_limit_bytes=60 * 2**20),
    )(gram, pair)


def shards(piv_cols, trail_cols, row_end, parent_of):
    parent = jnp.broadcast_to(parent_of[:, None], (8, 128))
    gram, pair = reduce_gram(piv_cols, trail_cols, row_end, parent)
    return factor(gram, pair)


def solution(mesh):
    return jax.shard_map(
        shards,
        mesh=mesh,
        in_specs=(P("sub", None, "front"), P("sub", None, "front"), P("sub", None), P("sub")),
        out_specs=(P(None, None, "front"), P(None, None, "front")),
        check_vma=False,
    )
```

```python
import jax
import jax.numpy as jnp
from jax import lax
from jax.experimental import pallas as pl
from jax.experimental.pallas import tpu as pltpu
from jax.sharding import PartitionSpec as P

F32 = jnp.float32
BF = jnp.bfloat16
HI = lax.Precision.HIGHEST
MESH = pl.DeviceIdType.MESH
LIVE = 1280
N = 1024
T = 1024
COLORS = 6
HALVINGS = 4
PIVOT_ROWS = (384,) * 6
TRAIL_ROWS = (1408,) * 4 + (1280,) * 2


def dims_of(sub):
    x, y, z = sub % 4, (sub // 4) % 4, sub // 16
    partner, side = [], []
    for kind in range(2):
        for coord, stride in ((x, 1), (y, 4), (z, 16)):
            if kind == 0:
                other, bit = coord + 1 - 2 * (coord % 2), ((coord + 1) // 2) % 2
            else:
                other, bit = 3 - coord, coord // 2
            partner.append(sub + (other - coord) * stride)
            side.append(bit)
    return partner, side


def rows_at(start, size):
    return pl.ds(pl.multiple_of(start, 8), size)


def step_of(h):
    return h if h <= 96 else max(d for d in range(8, 97, 8) if h % d == 0)


class Exchange:
    def __init__(self, rows, g, work, inbox, total, send, recv, partner, side, weights):
        self.rows, self.g, self.work, self.inbox, self.total = rows, g, work, inbox, total
        self.send, self.recv, self.partner, self.side, self.weights = send, recv, partner, side, weights
        self.off = [sum(rows[:q]) for q in range(COLORS)]
        self.rel = [0] * COLORS
        self.flying = {}

    def size(self, q, s):
        return self.rows[q] >> (min(s, HALVINGS - 1) + 1)

    def describe(self, q, s, slot, src, dst):
        d = (q + s) % 6
        self.flying[q, slot] = pltpu.make_async_remote_copy(
            src, dst, self.send.at[q, slot], self.recv.at[q, slot],
            device_id={"sub": self.partner[d]}, device_id_type=MESH)

    def describe_scatter(self, q, s):
        d, h = (q + s) % 6, self.size(q, s)
        if s == 0:
            src = self.g.at[rows_at(self.off[q] + (1 - self.side[d]) * h, h), :]
            dst = self.inbox[0].at[q, pl.ds(0, h), :]
        else:
            start = self.rel[q] + ((1 - self.side[d]) * h if s < HALVINGS else 0)
            src = self.work.at[q, :, rows_at(start, h), :]
            dst = self.inbox[s].at[q, :, pl.ds(0, h), :]
        self.describe(q, s, s, src, dst)

    def start_scatter(self, q, s):
        self.describe_scatter(q, s)
        self.flying[q, s].start()

    def scatter(self, q, s):
        d, h = (q + s) % 6, self.size(q, s)
        step = step_of(h)
        if s < HALVINGS:
            self.off[q] = self.off[q] + self.side[d] * h
            if s:
                self.rel[q] = self.rel[q] + self.side[d] * h
        off, rel, work, inbox = self.off[q], self.rel[q], self.work, self.inbox[s]
        self.flying[q, s].wait()
        if s == 0:
            weights = self.weights(q)

        @pl.loop(0, h // step)
        def _(i):
            there = rows_at(i * step, step)
            here = rows_at(rel + i * step, step)
            if s == 0:
                mine, theirs = self.g[rows_at(off + i * step, step), :], inbox[q, there, :]
                for p in range(2):
                    work[q, p, there, :] = mine * weights[p][0] + theirs * weights[p][1]
            elif s < 5:
                work[q, :, here, :] = work[q, :, here, :] + inbox[q, :, there, :]
            else:
                self.total[:, rows_at(off + i * step, step), :] = work[q, :, here, :] + inbox[q, :, there, :]

        if s < 5:
            self.start_scatter(q, s + 1)
        else:
            self.start_gather(q, HALVINGS - 1)

    def describe_gather(self, q, s):
        rows = self.total.at[:, rows_at(self.off[q], self.size(q, s)), :]
        self.describe(q, s, 6 + s, rows, rows)

    def start_gather(self, q, s):
        self.describe_gather(q, s)
        self.flying[q, 6 + s].start()

    def gather(self, q, s):
        d, h = (q + s) % 6, self.size(q, s)
        self.flying[q, 6 + s].wait()
        theirs = self.off[q] + (1 - 2 * self.side[d]) * h
        self.off[q] = self.off[q] - self.side[d] * h
        if s > 0:
            self.start_gather(q, s - 1)
        return theirs, h


def split(x):
    h = x.astype(BF)
    r = x - h.astype(F32)
    m = r.astype(BF)
    l = (r - m.astype(F32)).astype(BF)
    return h, m, l


def stack_rhs(x, count):
    h, m, l = split(x)
    return jnp.concatenate([h, m, h, l, m, h][:count], axis=0)


def stack_lhs(h, m, l=None):
    return jnp.concatenate([h, h, m] if l is None else [h, h, m, h, m, l], axis=1)


def dot(a, b):
    return lax.dot_general(a, b, (((1,), (0,)), ((), ())), preferred_element_type=F32)


def dot_t(a, b):
    return lax.dot_general(a, b, (((0,), (0,)), ((), ())), precision=HI, preferred_element_type=F32)


def spread(x):
    return jnp.broadcast_to(x, (8, 128))


def leaf(s, first, last):
    sub = lax.broadcasted_iota(jnp.int32, (8, 256), 0)
    for g in range(first, last):
        for p in range(2):
            rows = [s[p, pl.ds(8 * g + j, 8, stride=0), :] for j in range(8)]
            if g < 15:
                nxt = s[p, 8 * g + 8 : 8 * g + 16, :]
                cols = [spread(nxt[:, 8 * g + j : 8 * g + j + 1]) for j in range(8)]
            a = {(i, j): spread(rows[i][:, 8 * g + j : 8 * g + j + 1]) for i in range(8) for j in range(i, 8)}
            m, u = {}, {}
            for k in range(8):
                r = lax.rsqrt(a[k, k])
                for j in range(k + 1, 8):
                    u[k, j] = a[k, j] * r
                m[k, k] = r
                for c in range(k):
                    m[k, c] = m[k, c] * r
                for i in range(k + 1, 8):
                    for j in range(i, 8):
                        a[i, j] = a[i, j] - u[k, i] * u[k, j]
                    for c in range(k + 1):
                        t = u[k, i] * m[k, c]
                        m[i, c] = (m[i, c] - t) if (i, c) in m else -t
            done = []
            for k in range(8):
                lo = sum(m[k, j] * rows[j][:, :128] for j in range(k + 1))
                hi = sum(m[k, j] * rows[j][:, 128:] for j in range(k + 1))
                done.append(jnp.concatenate([lo, hi], axis=1))
            out = done[0]
            for k in range(1, 8):
                out = jnp.where(sub == k, done[k], out)
            s[p, 8 * g : 8 * g + 8, :] = out
            if g < 15:
                lo, hi = nxt[:, :128], nxt[:, 128:]
                for k in range(8):
                    l = sum(m[k, j] * cols[j] for j in range(k + 1))
                    lo = lo - l * done[k][:, :128]
                    hi = hi - l * done[k][:, 128:]
                s[p, 8 * g + 8 : 8 * g + 16, :] = jnp.concatenate([lo, hi], axis=1)
            if g < 14:
                upd = dot_t(out[:, :128], out)
                s[p, 8 * g + 16 :, :] = s[p, 8 * g + 16 :, :] - upd[8 * g + 16 :, :]


def block_of(core, b):
    t, o = 2 * core + b // 9, b % 9
    c = (o + t) // 8
    return t + c * (7 - 2 * t), (1 - c) * (t + o) + c * (o - 1)


def main_kernel(piv, trail, row_end, parent, trail_out, lhs_out, w_out, piv_out,
                half_in, cols_in, turned, gp, wp, totp, pair, gt, wt, ut, u, s, rhs, lhs, low, w,
                p0, p1, p2, p3, p4, p5, t0, t1, t2, t3, t4, t5, pids,
                in_sem, sendp, recvp, sendt, recvt, psend, precv, dsend, drecv, hsend, hrecv, out_sem, lhs_sem):
    front = lax.axis_index("front")
    sub = lax.axis_index("sub")
    partner, side = dims_of(sub)

    local = [pltpu.make_async_copy(piv.at[0, pl.ds(0, LIVE), :], half_in.at[front], in_sem.at[0])]
    for j in range(4):
        local.append(pltpu.make_async_copy(
            trail.at[0, pl.ds(0, LIVE), pl.ds(256 * j, 256)], cols_in.at[j], in_sem.at[1 + j]))
    for copy in local:
        copy.start()

    barrier = pltpu.get_barrier_semaphore()
    for d in range(6):
        pl.semaphore_signal(barrier, inc=1, device_id={"sub": partner[d]}, device_id_type=MESH)
    pl.semaphore_signal(barrier, inc=1, device_id={"front": 1 - front}, device_id_type=MESH)
    pl.semaphore_wait(barrier, 7)

    half = pltpu.make_async_remote_copy(
        piv.at[0, pl.ds(0, LIVE), :], half_in.at[front], hsend, hrecv,
        device_id={"front": 1 - front}, device_id_type=MESH)
    half.start()
    pid_copies = []
    for q in range(COLORS):
        copy = pltpu.make_async_remote_copy(
            parent, pids.at[q], psend.at[q], precv.at[q],
            device_id={"sub": partner[q]}, device_id_type=MESH)
        copy.start()
        pid_copies.append(copy)

    def weights(q):
        own, other = parent[0:1, 0:1], pids[q, 0:1, 0:1]
        return [((own == p).astype(F32), (other == p).astype(F32)) for p in range(2)]

    pivots = Exchange(PIVOT_ROWS, gp, wp, (p0, p1, p2, p3, p4, p5), totp, sendp, recvp, partner, side, weights)
    trails = Exchange(TRAIL_ROWS, gt, wt, (t0, t1, t2, t3, t4, t5), ut, sendt, recvt, partner, side, weights)

    row_ids = lax.broadcasted_iota(jnp.int32, (LIVE, 128), 0)

    def block(i):
        return pl.ds(pl.multiple_of(i * 128, 128), 128)

    def turn(which):
        @pl.loop(0, 4)
        def _(b):
            value = half_in[which, :, block(b)].astype(F32)
            value = jnp.where(row_ids < row_end[0, which * 4 + b], value, 0.0)
            turned[block(which * 4 + b), :] = jnp.transpose(value).astype(BF)

    local[0].wait()
    turn(front)
    half.wait()
    turn(1 - front)

    for q in range(COLORS):
        @pl.loop(0, 3)
        def _(e):
            i, j = block_of(front, q * 3 + e)
            gp[block(q * 3 + e), :] = dot(turned[block(i), :], half_in[j // 4, :, block(j % 4)])

        pivots.start_scatter(q, 0)
    for copy in pid_copies:
        copy.wait()

    def trail_gram(j):
        local[1 + j].wait()

        @pl.loop(0, 4)
        def _(i):
            rows = pl.ds(pl.multiple_of(i * 256, 256), 256)
            value = dot(turned[rows, :], cols_in[j])
            gt[rows_at(2 * j * 1024 + i * 256, 256), :] = value[:, :128]
            gt[rows_at((2 * j + 1) * 1024 + i * 256, 256), :] = value[:, 128:]

    for st in range(6):
        if st < 4:
            trail_gram(st)
        for q in range(COLORS):
            pivots.scatter(q, st)

    to_pair = []

    def start_pair(q, k, start, size):
        rows = rows_at(start, size)
        copy = pltpu.make_async_remote_copy(
            totp.at[:, rows, :], pair.at[:, rows, :], dsend.at[q, k], drecv.at[q, k],
            device_id={"front": 1 - front}, device_id_type=MESH)
        copy.start()
        to_pair.append(copy)

    for q in range(COLORS):
        start_pair(q, 4, pivots.off[q], pivots.size(q, 3))
    for st in range(3, -1, -1):
        for q in range(COLORS):
            start, size = pivots.gather(q, st)
            start_pair(q, st, start, size)
        if st == 1:
            for q in range(COLORS):
                trails.start_scatter(q, 0)

    def place(core, src):
        @pl.loop(0, 18)
        def _(b):
            i, j = block_of(core, b)
            for p in range(2):
                u[p, block(i), block(j)] = src[p, block(b), :]

    place(front, totp)
    for copy in to_pair:
        copy.wait()
    place(1 - front, pair)

    outs = []

    def trail_out_copy():
        copy = pltpu.make_async_copy(ut, trail_out, out_sem.at[0])
        copy.start()
        outs.append(copy)

    def tick(n):
        for q in range(COLORS):
            if n < 6:
                trails.scatter(q, n)
            else:
                trails.gather(q, 9 - n)
        if n == 9:
            trail_out_copy()

    plan = {0: (0, 1), 1: (1, 0), 2: (1, 2), 3: (2, 0), 4: (2, 1), 5: (2, 2), 6: (3, 0), 7: (3, 2), 8: (4, 2), 9: (6, 1)}

    def ticks(k, place_):
        for n, (kk, where) in plan.items():
            if where == place_:
                yield n, kk

    ri = lax.broadcasted_iota(jnp.int32, (128, 128), 0)
    ci = lax.broadcasted_iota(jnp.int32, (128, 128), 1)

    states = {}
    for n in range(10):
        states[n] = (list(trails.off), list(trails.rel))
        for q in range(COLORS):
            st = n if n < 6 else 9 - n
            d, h = (q + st) % 6, trails.size(q, st)
            if n < HALVINGS:
                trails.off[q] = trails.off[q] + side[d] * h
                if n:
                    trails.rel[q] = trails.rel[q] + side[d] * h
            elif n >= 6:
                trails.off[q] = trails.off[q] - side[d] * h

    def rebuild(n):
        off, rel = states[n]
        trails.off, trails.rel = list(off), list(rel)
        trails.flying = {}
        for q in range(COLORS):
            if n < 6:
                trails.describe_scatter(q, n)
            else:
                trails.describe_gather(q, 9 - n)

    def run_ticks(k, where):
        for n, kk in ticks(k, where):
            @pl.when(k == kk)
            def _():
                rebuild(n)
                tick(n)

    @pl.loop(0, 8)
    def _(k):
        rs = block(k)
        for p in range(2):
            d = u[p, rs, rs]
            s[p, :, :128] = jnp.where(ri <= ci, d, jnp.transpose(d))
            s[p, :, 128:] = (ri == ci).astype(F32)
        leaf(s, 0, 8)
        run_ticks(k, 0)
        leaf(s, 8, 16)
        run_ticks(k, 1)
        for p in range(2):
            wh, wm, wl = split(s[p, :, 128:])
            w[p, k] = jnp.concatenate([wh, wm], axis=1)
            wst = stack_lhs(wh, wm, wl)
            for t in range(2):
                cs = pl.ds(t * 512, 512)
                r = dot(wst, stack_rhs(u[p, rs, cs], 6))
                cols = lax.broadcasted_iota(jnp.int32, (128, 512), 1) + t * 512
                r = jnp.where(cols >= (k + 1) * 128, r, 0.0)
                u[p, rs, cs] = r
                rhs[p, :, cs] = stack_rhs(r, 6)
                th, tm, tl = split(jnp.transpose(r))
                lhs[p, k, cs, :] = jnp.concatenate([th, tm], axis=1)
                low[p, cs, :] = tl
            u[p, rs, rs] = jnp.where(ri <= ci, s[p, :, :128], 0.0)
            pltpu.make_async_copy(lhs.at[p, k], lhs_out.at[p, k], lhs_sem.at[p, k]).start()

        @pl.loop((k + 1) // 2, 4)
        def _(c):
            rows = pl.ds(pl.multiple_of(c * 256, 256), 256)
            for p in range(2):
                l = lhs[p, k, rows, :]
                l = stack_lhs(l[:, :128], l[:, 128:], low[p, rows, :])

                @pl.loop(c, 4)
                def _(j):
                    cols = pl.ds(pl.multiple_of(j * 256, 256), 256)
                    u[p, rows, cols] = u[p, rows, cols] - dot(l, rhs[p, :, cols])

        run_ticks(k, 2)

    own = pl.ds(pl.multiple_of(front * 512, 512), 512)
    last = [pltpu.make_async_copy(ut, trail_out, out_sem.at[0]), pltpu.make_async_copy(w, w_out, out_sem.at[1])]
    last[1].start()
    for p in range(2):
        copy = pltpu.make_async_copy(u.at[p, :, own], piv_out.at[p], out_sem.at[2 + p])
        copy.start()
        last.append(copy)
        for k in range(8):
            last.append(pltpu.make_async_copy(lhs.at[p, k], lhs_out.at[p, k], lhs_sem.at[p, k]))
    for copy in last:
        copy.wait()


def main_call(piv, trail, row_end, parent):
    dma = pltpu.SemaphoreType.DMA

    def inbox(rows):
        top = max(rows)
        sizes = [top >> (min(s, HALVINGS - 1) + 1) for s in range(6)]
        return [pltpu.VMEM((COLORS, sizes[0], 128), F32)] + [pltpu.VMEM((COLORS, 2, h, 128), F32) for h in sizes[1:]]

    return pl.pallas_call(
        main_kernel,
        out_shape=(
            jax.ShapeDtypeStruct((2, 8 * N, 128), F32),
            jax.ShapeDtypeStruct((2, 8, N, 256), BF),
            jax.ShapeDtypeStruct((2, 8, 128, 256), BF),
            jax.ShapeDtypeStruct((2, N, 512), F32),
        ),
        in_specs=[
            pl.BlockSpec(memory_space=pl.ANY),
            pl.BlockSpec(memory_space=pl.ANY),
            pl.BlockSpec(memory_space=pltpu.SMEM),
            pl.BlockSpec(memory_space=pltpu.VMEM),
        ],
        out_specs=[pl.BlockSpec(memory_space=pl.ANY)] * 4,
        scratch_shapes=[
            pltpu.VMEM((2, LIVE, 512), BF),
            pltpu.VMEM((4, LIVE, 256), BF),
            pltpu.VMEM((N, LIVE), BF),
            pltpu.VMEM((2304, 128), F32),
            pltpu.VMEM((COLORS, 2, 192, 128), F32),
            pltpu.VMEM((2, 2304, 128), F32),
            pltpu.VMEM((2, 2304, 128), F32),
            pltpu.VMEM((8 * N, 128), F32),
            pltpu.VMEM((COLORS, 2, 704, 128), F32),
            pltpu.VMEM((2, 8 * N, 128), F32),
            pltpu.VMEM((2, N, N), F32),
            pltpu.VMEM((2, 128, 256), F32),
            pltpu.VMEM((2, 768, N), BF),
            pltpu.VMEM((2, 8, N, 256), BF),
            pltpu.VMEM((2, N, 128), BF),
            pltpu.VMEM((2, 8, 128, 256), BF),
            *inbox(PIVOT_ROWS),
            *inbox(TRAIL_ROWS),
            pltpu.VMEM((COLORS, 8, 128), jnp.int32),
            dma((5,)),
            dma((COLORS, 10)),
            dma((COLORS, 10)),
            dma((COLORS, 10)),
            dma((COLORS, 10)),
            dma((COLORS,)),
            dma((COLORS,)),
            dma((COLORS, 5)),
            dma((COLORS, 5)),
            dma,
            dma,
            dma((4,)),
            dma((2, 8)),
        ],
        compiler_params=pltpu.CompilerParams(
            collective_id=0, has_side_effects=True, vmem_limit_bytes=67043328),
    )(piv, trail, row_end, parent)


def solve_kernel(trail, lhs, w, piv, r_trail, r_piv, v):
    r_piv[...] = piv[...]
    for p in range(2):
        for j in range(2):
            v[p, :, 128 * j : 128 * j + 128] = trail[p, j]

    @pl.loop(0, 8)
    def _(k):
        rows = pl.ds(pl.multiple_of(k * 128, 128), 128)
        right = []
        for p in range(2):
            wk = w[p, k]
            r = dot(stack_lhs(wk[:, :128], wk[:, 128:]), stack_rhs(v[p, rows, :], 3))
            v[p, rows, :] = r
            right.append(stack_rhs(r, 3))

        @pl.loop((k + 1) // 2, 4)
        def _(c):
            chunk = pl.ds(pl.multiple_of(c * 256, 256), 256)
            for p in range(2):
                l = lhs[p, k, chunk, :]
                v[p, chunk, :] = v[p, chunk, :] - dot(stack_lhs(l[:, :128], l[:, 128:]), right[p])

    r_trail[...] = v[...]


def solve_trail(trail, lhs, w, piv):
    whole = pl.Buffered(1)
    return pl.pallas_call(
        solve_kernel,
        grid=(4,),
        out_shape=(jax.ShapeDtypeStruct((2, N, T), F32), jax.ShapeDtypeStruct((2, N, 512), F32)),
        in_specs=[
            pl.BlockSpec((2, 2, N, 128), lambda c: (0, c, 0, 0)),
            pl.BlockSpec((2, 8, N, 256), lambda c: (0, 0, 0, 0), pipeline_mode=whole),
            pl.BlockSpec((2, 8, 128, 256), lambda c: (0, 0, 0, 0), pipeline_mode=whole),
            pl.BlockSpec((2, 256, 512), lambda c: (0, c, 0)),
        ],
        out_specs=[
            pl.BlockSpec((2, N, 256), lambda c: (0, 0, c)),
            pl.BlockSpec((2, 256, 512), lambda c: (0, c, 0)),
        ],
        scratch_shapes=[pltpu.VMEM((2, N, 256), F32)],
        compiler_params=pltpu.CompilerParams(vmem_limit_bytes=60 * 2**20),
    )(trail.reshape(2, 8, N, 128), lhs, w, piv)


def shards(piv_cols, trail_cols, row_end, parent_of):
    parent = jnp.broadcast_to(parent_of[:, None], (8, 128))
    trail, lhs, w, piv = main_call(piv_cols, trail_cols, row_end, parent)
    r_trail, r_pivot = solve_trail(trail, lhs, w, piv)
    return r_pivot, r_trail


def solution(mesh):
    return jax.shard_map(
        shards,
        mesh=mesh,
        in_specs=(P("sub", None, "front"), P("sub", None, "front"), P("sub", None), P("sub")),
        out_specs=(P(None, None, "front"), P(None, None, "front")),
        check_vma=False,
    )
```

```python
import jax
import jax.numpy as jnp
from jax import lax
from jax.experimental import pallas as pl
from jax.experimental.pallas import tpu as pltpu
from jax.sharding import PartitionSpec as P

F32 = jnp.float32
BF = jnp.bfloat16
MESH = pl.DeviceIdType.MESH
LIVE = 1280
N = 1024
T = 1024
COLORS = 6
HALVINGS = 4
PIVOT_ROWS = (384,) * 6
TRAIL_ROWS = (1408,) * 4 + (1280,) * 2


def dims_of(sub):
    x, y, z = sub % 4, (sub // 4) % 4, sub // 16
    partner, side = [], []
    for kind in range(2):
        for coord, stride in ((x, 1), (y, 4), (z, 16)):
            if kind == 0:
                other, bit = coord + 1 - 2 * (coord % 2), ((coord + 1) // 2) % 2
            else:
                other, bit = 3 - coord, coord // 2
            partner.append(sub + (other - coord) * stride)
            side.append(bit)
    return partner, side


def rows_at(start, size):
    return pl.ds(pl.multiple_of(start, 8), size)


def step_of(h):
    return h if h <= 96 else max(d for d in range(8, 97, 8) if h % d == 0)


class Exchange:
    def __init__(self, rows, g, work, inbox, total, send, recv, partner, side, weights):
        self.rows, self.g, self.work, self.inbox, self.total = rows, g, work, inbox, total
        self.send, self.recv, self.partner, self.side, self.weights = send, recv, partner, side, weights
        self.off = [sum(rows[:q]) for q in range(COLORS)]
        self.rel = [0] * COLORS
        self.flying = {}

    def size(self, q, s):
        return self.rows[q] >> (min(s, HALVINGS - 1) + 1)

    def describe(self, q, s, slot, src, dst):
        d = (q + s) % 6
        self.flying[q, slot] = pltpu.make_async_remote_copy(
            src, dst, self.send.at[q, slot], self.recv.at[q, slot],
            device_id={"sub": self.partner[d]}, device_id_type=MESH)

    def describe_scatter(self, q, s):
        d, h = (q + s) % 6, self.size(q, s)
        if s == 0:
            src = self.g.at[rows_at(self.off[q] + (1 - self.side[d]) * h, h), :]
            dst = self.inbox[0].at[q, pl.ds(0, h), :]
        else:
            start = self.rel[q] + ((1 - self.side[d]) * h if s < HALVINGS else 0)
            src = self.work.at[q, :, rows_at(start, h), :]
            dst = self.inbox[s].at[q, :, pl.ds(0, h), :]
        self.describe(q, s, s, src, dst)

    def start_piece(self, i):
        for q in range(COLORS):
            h = self.size(q, 0)
            start = self.off[q] + (1 - self.side[q]) * h + i * (h // 4)
            pltpu.make_async_remote_copy(
                self.g.at[rows_at(start, h // 4), :], self.inbox[0].at[q, pl.ds(i * (h // 4), h // 4), :],
                self.send.at[q, 0], self.recv.at[q, 0],
                device_id={"sub": self.partner[q]}, device_id_type=MESH).start()

    def start_scatter(self, q, s):
        self.describe_scatter(q, s)
        self.flying[q, s].start()

    def scatter(self, q, s):
        d, h = (q + s) % 6, self.size(q, s)
        step = step_of(h)
        if s < HALVINGS:
            self.off[q] = self.off[q] + self.side[d] * h
            if s:
                self.rel[q] = self.rel[q] + self.side[d] * h
        off, rel, work, inbox = self.off[q], self.rel[q], self.work, self.inbox[s]
        self.flying[q, s].wait()
        if s == 0:
            weights = self.weights(q)

        @pl.loop(0, h // step)
        def _(i):
            there = rows_at(i * step, step)
            here = rows_at(rel + i * step, step)
            if s == 0:
                mine, theirs = self.g[rows_at(off + i * step, step), :], inbox[q, there, :]
                for p in range(2):
                    work[q, p, there, :] = mine * weights[p][0] + theirs * weights[p][1]
            elif s < 5:
                work[q, :, here, :] = work[q, :, here, :] + inbox[q, :, there, :]
            else:
                self.total[:, rows_at(off + i * step, step), :] = work[q, :, here, :] + inbox[q, :, there, :]

        if s < 5:
            self.start_scatter(q, s + 1)
        else:
            self.start_gather(q, HALVINGS - 1)

    def describe_gather(self, q, s):
        rows = self.total.at[:, rows_at(self.off[q], self.size(q, s)), :]
        self.describe(q, s, 6 + s, rows, rows)

    def start_gather(self, q, s):
        self.describe_gather(q, s)
        self.flying[q, 6 + s].start()

    def gather(self, q, s):
        d, h = (q + s) % 6, self.size(q, s)
        self.flying[q, 6 + s].wait()
        theirs = self.off[q] + (1 - 2 * self.side[d]) * h
        self.off[q] = self.off[q] - self.side[d] * h
        if s > 0:
            self.start_gather(q, s - 1)
        return theirs, h


def split(x):
    h = x.astype(BF)
    r = x - h.astype(F32)
    m = r.astype(BF)
    l = (r - m.astype(F32)).astype(BF)
    return h, m, l


def stack_rhs(x, count):
    h, m, l = split(x)
    return jnp.concatenate([h, m, h, l, m, h][:count], axis=0)


def stack_lhs(h, m, l=None):
    return jnp.concatenate([h, h, m] if l is None else [h, h, m, h, m, l], axis=1)


def dot(a, b):
    return lax.dot_general(a, b, (((1,), (0,)), ((), ())), preferred_element_type=F32)


def spread(x):
    return jnp.broadcast_to(x, (8, 128))


def low_dot(out):
    h = out.astype(BF).astype(F32)
    r = out - h
    m = r.astype(BF).astype(F32)
    l = r - m
    left = jnp.concatenate([h, h, m, h, m, l], axis=0)[:, :128].astype(BF)
    right = jnp.concatenate([h, m, h, l, m, h], axis=0).astype(BF)
    return lax.dot_general(left, right, (((0,), (0,)), ((), ())), preferred_element_type=F32)


def leaf(s, first, last):
    sub = lax.broadcasted_iota(jnp.int32, (8, 256), 0)
    for g in range(first, last):
        for p in range(2):
            rows = [s[p, pl.ds(8 * g + j, 8, stride=0), :] for j in range(8)]
            if g < 15:
                nxt = s[p, 8 * g + 8 : 8 * g + 16, :]
                cols = [spread(nxt[:, 8 * g + j : 8 * g + j + 1]) for j in range(8)]
            a = {(i, j): spread(rows[i][:, 8 * g + j : 8 * g + j + 1]) for i in range(8) for j in range(i, 8)}
            m, u = {}, {}
            for k in range(8):
                r = lax.rsqrt(a[k, k])
                for j in range(k + 1, 8):
                    u[k, j] = a[k, j] * r
                m[k, k] = r
                for c in range(k):
                    m[k, c] = m[k, c] * r
                for i in range(k + 1, 8):
                    for j in range(i, 8):
                        a[i, j] = a[i, j] - u[k, i] * u[k, j]
                    for c in range(k + 1):
                        t = u[k, i] * m[k, c]
                        m[i, c] = (m[i, c] - t) if (i, c) in m else -t
            done = []
            for k in range(8):
                lo = sum(m[k, j] * rows[j][:, :128] for j in range(k + 1))
                hi = sum(m[k, j] * rows[j][:, 128:] for j in range(k + 1))
                done.append(jnp.concatenate([lo, hi], axis=1))
            out = done[0]
            for k in range(1, 8):
                out = jnp.where(sub == k, done[k], out)
            s[p, 8 * g : 8 * g + 8, :] = out
            if g < 15:
                lo, hi = nxt[:, :128], nxt[:, 128:]
                for k in range(8):
                    l = sum(m[k, j] * cols[j] for j in range(k + 1))
                    lo = lo - l * done[k][:, :128]
                    hi = hi - l * done[k][:, 128:]
                s[p, 8 * g + 8 : 8 * g + 16, :] = jnp.concatenate([lo, hi], axis=1)
            if g < 14:
                upd = low_dot(out)
                s[p, 8 * g + 16 :, :] = s[p, 8 * g + 16 :, :] - upd[8 * g + 16 :, :]


def block_of(core, b):
    t, o = 2 * core + b // 9, b % 9
    c = (o + t) // 8
    return t + c * (7 - 2 * t), (1 - c) * (t + o) + c * (o - 1)


def main_kernel(piv, trail, row_end, parent, trail_out, lhs_out, w_out, piv_out,
                half_in, cols_in, turned, gp, wp, totp, pair, gt, wt, ut, u, s, rhs, lhs, low, w,
                p0, p1, p2, p3, p4, p5, t0, t1, t2, t3, t4, t5, pids,
                in_sem, sendp, recvp, sendt, recvt, psend, precv, dsend, drecv, hsend, hrecv, out_sem, lhs_sem, trail_sem):
    front = lax.axis_index("front")
    sub = lax.axis_index("sub")
    partner, side = dims_of(sub)

    local = [pltpu.make_async_copy(piv.at[0, pl.ds(0, LIVE), :], half_in.at[front], in_sem.at[0])]
    for j in range(4):
        local.append(pltpu.make_async_copy(
            trail.at[0, pl.ds(0, LIVE), pl.ds(256 * j, 256)], cols_in.at[j], in_sem.at[1 + j]))
    for copy in local:
        copy.start()

    barrier = pltpu.get_barrier_semaphore()
    for d in range(6):
        pl.semaphore_signal(barrier, inc=1, device_id={"sub": partner[d]}, device_id_type=MESH)
    pl.semaphore_signal(barrier, inc=1, device_id={"front": 1 - front}, device_id_type=MESH)
    pl.semaphore_wait(barrier, 7)

    half = pltpu.make_async_remote_copy(
        piv.at[0, pl.ds(0, LIVE), :], half_in.at[front], hsend, hrecv,
        device_id={"front": 1 - front}, device_id_type=MESH)
    half.start()
    pid_copies = []
    for q in range(COLORS):
        copy = pltpu.make_async_remote_copy(
            parent, pids.at[q], psend.at[q], precv.at[q],
            device_id={"sub": partner[q]}, device_id_type=MESH)
        copy.start()
        pid_copies.append(copy)

    def weights(q):
        own, other = parent[0:1, 0:1], pids[q, 0:1, 0:1]
        return [((own == p).astype(F32), (other == p).astype(F32)) for p in range(2)]

    pivots = Exchange(PIVOT_ROWS, gp, wp, (p0, p1, p2, p3, p4, p5), totp, sendp, recvp, partner, side, weights)
    trails = Exchange(TRAIL_ROWS, gt, wt, (t0, t1, t2, t3, t4, t5), ut, sendt, recvt, partner, side, weights)

    row_ids = lax.broadcasted_iota(jnp.int32, (LIVE, 128), 0)

    def block(i):
        return pl.ds(pl.multiple_of(i * 128, 128), 128)

    def turn(which):
        @pl.loop(0, 4)
        def _(b):
            value = half_in[which, :, block(b)].astype(F32)
            value = jnp.where(row_ids < row_end[0, which * 4 + b], value, 0.0)
            turned[block(which * 4 + b), :] = jnp.transpose(value).astype(BF)

    local[0].wait()
    turn(front)
    half.wait()
    turn(1 - front)

    for strip in range(2):
        t = 2 * front + strip
        left = jnp.concatenate([turned[block(t), :], turned[block(7 - t), :]], axis=0)

        @pl.loop(0, 4)
        def _(c):
            value = dot(left, half_in[c // 2, :, pl.ds(pl.multiple_of((c % 2) * 256, 256), 256)])
            for e in range(2):
                col = 2 * c + e
                upper = (col - t + 8) // 8
                slot = upper * (strip * 9 + col - t) + (1 - upper) * 18
                gp[block(slot), :] = value[:128, 128 * e : 128 * e + 128]
                upper = (col + t + 1) // 8
                slot = upper * (strip * 9 + col + 1) + (1 - upper) * 18
                gp[block(slot), :] = value[128:, 128 * e : 128 * e + 128]

        for q in range(3 * strip, 3 * strip + 3):
            pivots.start_scatter(q, 0)
    for copy in pid_copies:
        copy.wait()

    def trail_gram(j):
        local[1 + j].wait()

        value = dot(turned[...], cols_in[j])
        gt[2 * j * 1024 : (2 * j + 1) * 1024, :] = value[:, :128]
        gt[(2 * j + 1) * 1024 : (2 * j + 2) * 1024, :] = value[:, 128:]

    for st in range(6):
        if st < 2:
            trail_gram(2 * st)
            trail_gram(2 * st + 1)
        for q in range(COLORS):
            pivots.scatter(q, st)
        if st >= 2:
            trails.start_piece(st - 2)

    to_pair = []

    def start_pair(q, k, start, size):
        rows = rows_at(start, size)
        copy = pltpu.make_async_remote_copy(
            totp.at[:, rows, :], pair.at[:, rows, :], dsend.at[q, k], drecv.at[q, k],
            device_id={"front": 1 - front}, device_id_type=MESH)
        copy.start()
        to_pair.append(copy)

    for q in range(COLORS):
        start_pair(q, 4, pivots.off[q], pivots.size(q, 3))
    for st in range(3, -1, -1):
        for q in range(COLORS):
            start, size = pivots.gather(q, st)
            start_pair(q, st, start, size)
        if st == 1:
            for q in range(COLORS):
                trails.describe_scatter(q, 0)
            for q in range(COLORS):
                trails.scatter(q, 0)

    def place(core, src):
        @pl.loop(0, 18)
        def _(b):
            i, j = block_of(core, b)
            for p in range(2):
                u[p, block(i), block(j)] = src[p, block(b), :]

    place(front, totp)
    for copy in to_pair:
        copy.wait()
    place(1 - front, pair)

    def trail_copy(q, part):
        off, h = states[9][0][q], trails.size(q, 0)
        rows = rows_at(off if part == 0 else off + (1 - 2 * side[q]) * h, h)
        return pltpu.make_async_copy(ut.at[:, rows, :], trail_out.at[:, rows, :], trail_sem.at[q, part])

    def tick(n):
        for q in range(COLORS):
            if n < 6:
                trails.scatter(q, n)
            else:
                trails.gather(q, 9 - n)
            if n >= 8:
                trail_copy(q, n - 8).start()

    plan = {1: (0, 3), 2: (1, 2), 3: (1, 5), 4: (2, 3), 5: (3, 0), 6: (3, 4), 7: (4, 3), 8: (5, 5), 9: (7, 5)}

    def ticks(k, place_):
        for n, (kk, where) in plan.items():
            if where == place_:
                yield n, kk

    ri = lax.broadcasted_iota(jnp.int32, (128, 128), 0)
    ci = lax.broadcasted_iota(jnp.int32, (128, 128), 1)

    states = {}
    for n in range(1, 10):
        states[n] = (list(trails.off), list(trails.rel))
        for q in range(COLORS):
            st = n if n < 6 else 9 - n
            d, h = (q + st) % 6, trails.size(q, st)
            if n < HALVINGS:
                trails.off[q] = trails.off[q] + side[d] * h
                if n:
                    trails.rel[q] = trails.rel[q] + side[d] * h
            elif n >= 6:
                trails.off[q] = trails.off[q] - side[d] * h

    def rebuild(n):
        off, rel = states[n]
        trails.off, trails.rel = list(off), list(rel)
        trails.flying = {}
        for q in range(COLORS):
            if n < 6:
                trails.describe_scatter(q, n)
            else:
                trails.describe_gather(q, 9 - n)

    def run_ticks(k, where):
        for n, kk in ticks(k, where):
            @pl.when(k == kk)
            def _():
                rebuild(n)
                tick(n)

    @pl.loop(0, 8)
    def _(k):
        rs = block(k)
        for p in range(2):
            d = u[p, rs, rs]
            s[p, :, :128] = jnp.where(ri <= ci, d, jnp.transpose(d))
            s[p, :, 128:] = (ri == ci).astype(F32)
        for part in range(4):
            leaf(s, 4 * part, 4 * part + 4)
            run_ticks(k, part)
        for p in range(2):
            wh, wm, wl = split(s[p, :, 128:])
            w[p, k] = jnp.concatenate([wh, wm], axis=1)
            wst = stack_lhs(wh, wm, wl)
            for t in range(2):
                cs = pl.ds(t * 512, 512)
                r = dot(wst, stack_rhs(u[p, rs, cs], 6))
                cols = lax.broadcasted_iota(jnp.int32, (128, 512), 1) + t * 512
                r = jnp.where(cols >= (k + 1) * 128, r, 0.0)
                u[p, rs, cs] = r
                rhs[p, :, cs] = stack_rhs(r, 6)
                th, tm, tl = split(jnp.transpose(r))
                lhs[p, k, cs, :] = jnp.concatenate([th, tm], axis=1)
                low[p, cs, :] = tl
            u[p, rs, rs] = jnp.where(ri <= ci, s[p, :, :128], 0.0)
            pltpu.make_async_copy(lhs.at[p, k], lhs_out.at[p, k], lhs_sem.at[p, k]).start()

        run_ticks(k, 4)

        @pl.loop((k + 1) // 2, 4)
        def _(c):
            rows = pl.ds(pl.multiple_of(c * 256, 256), 256)
            for p in range(2):
                l = lhs[p, k, rows, :]
                l = stack_lhs(l[:, :128], l[:, 128:], low[p, rows, :])

                @pl.loop(c, 4)
                def _(j):
                    cols = pl.ds(pl.multiple_of(j * 256, 256), 256)
                    u[p, rows, cols] = u[p, rows, cols] - dot(l, rhs[p, :, cols])

        run_ticks(k, 5)

    own = pl.ds(pl.multiple_of(front * 512, 512), 512)
    last = [pltpu.make_async_copy(w, w_out, out_sem.at[0])]
    last[0].start()
    for q in range(COLORS):
        last += [trail_copy(q, 0), trail_copy(q, 1)]
    for p in range(2):
        copy = pltpu.make_async_copy(u.at[p, :, own], piv_out.at[p], out_sem.at[1 + p])
        copy.start()
        last.append(copy)
        for k in range(8):
            last.append(pltpu.make_async_copy(lhs.at[p, k], lhs_out.at[p, k], lhs_sem.at[p, k]))
    for copy in last:
        copy.wait()


def main_call(piv, trail, row_end, parent):
    dma = pltpu.SemaphoreType.DMA

    def inbox(rows):
        top = max(rows)
        sizes = [top >> (min(s, HALVINGS - 1) + 1) for s in range(6)]
        return [pltpu.VMEM((COLORS, sizes[0], 128), F32)] + [pltpu.VMEM((COLORS, 2, h, 128), F32) for h in sizes[1:]]

    return pl.pallas_call(
        main_kernel,
        out_shape=(
            jax.ShapeDtypeStruct((2, 8 * N, 128), F32),
            jax.ShapeDtypeStruct((2, 8, N, 256), BF),
            jax.ShapeDtypeStruct((2, 8, 128, 256), BF),
            jax.ShapeDtypeStruct((2, N, 512), F32),
        ),
        in_specs=[
            pl.BlockSpec(memory_space=pl.ANY),
            pl.BlockSpec(memory_space=pl.ANY),
            pl.BlockSpec(memory_space=pltpu.SMEM),
            pl.BlockSpec(memory_space=pltpu.VMEM),
        ],
        out_specs=[pl.BlockSpec(memory_space=pl.ANY)] * 4,
        scratch_shapes=[
            pltpu.VMEM((2, LIVE, 512), BF),
            pltpu.VMEM((4, LIVE, 256), BF),
            pltpu.VMEM((N, LIVE), BF),
            pltpu.VMEM((2304 + 128, 128), F32),
            pltpu.VMEM((COLORS, 2, 192, 128), F32),
            pltpu.VMEM((2, 2304, 128), F32),
            pltpu.VMEM((2, 2304, 128), F32),
            pltpu.VMEM((8 * N, 128), F32),
            pltpu.VMEM((COLORS, 2, 704, 128), F32),
            pltpu.VMEM((2, 8 * N, 128), F32),
            pltpu.VMEM((2, N, N), F32),
            pltpu.VMEM((2, 128, 256), F32),
            pltpu.VMEM((2, 768, N), BF),
            pltpu.VMEM((2, 8, N, 256), BF),
            pltpu.VMEM((2, N, 128), BF),
            pltpu.VMEM((2, 8, 128, 256), BF),
            *inbox(PIVOT_ROWS),
            *inbox(TRAIL_ROWS),
            pltpu.VMEM((COLORS, 8, 128), jnp.int32),
            dma((5,)),
            dma((COLORS, 10)),
            dma((COLORS, 10)),
            dma((COLORS, 10)),
            dma((COLORS, 10)),
            dma((COLORS,)),
            dma((COLORS,)),
            dma((COLORS, 5)),
            dma((COLORS, 5)),
            dma,
            dma,
            dma((3,)),
            dma((2, 8)),
            dma((COLORS, 2)),
        ],
        compiler_params=pltpu.CompilerParams(
            collective_id=0, has_side_effects=True, vmem_limit_bytes=67043328),
    )(piv, trail, row_end, parent)


def solve_kernel(trail, lhs, w, piv, r_trail, r_piv, v):
    r_piv[...] = piv[...]
    for p in range(2):
        for j in range(4):
            v[p, :, 128 * j : 128 * j + 128] = trail[p, j]

    @pl.loop(0, 8)
    def _(k):
        rows = pl.ds(pl.multiple_of(k * 128, 128), 128)
        right = []
        for p in range(2):
            wk = w[p, k]
            r = dot(stack_lhs(wk[:, :128], wk[:, 128:]), stack_rhs(v[p, rows, :], 3))
            v[p, rows, :] = r
            right.append(stack_rhs(r, 3))

        @pl.loop((k + 1) // 2, 4)
        def _(c):
            chunk = pl.ds(pl.multiple_of(c * 256, 256), 256)
            for p in range(2):
                l = lhs[p, k, chunk, :]
                v[p, chunk, :] = v[p, chunk, :] - dot(stack_lhs(l[:, :128], l[:, 128:]), right[p])

    r_trail[...] = v[...]


def solve_trail(trail, lhs, w, piv):
    whole = pl.Buffered(1)
    return pl.pallas_call(
        solve_kernel,
        grid=(2,),
        out_shape=(jax.ShapeDtypeStruct((2, N, T), F32), jax.ShapeDtypeStruct((2, N, 512), F32)),
        in_specs=[
            pl.BlockSpec((2, 4, N, 128), lambda c: (0, c, 0, 0)),
            pl.BlockSpec((2, 8, N, 256), lambda c: (0, 0, 0, 0), pipeline_mode=whole),
            pl.BlockSpec((2, 8, 128, 256), lambda c: (0, 0, 0, 0), pipeline_mode=whole),
            pl.BlockSpec((2, 512, 512), lambda c: (0, c, 0)),
        ],
        out_specs=[
            pl.BlockSpec((2, N, 512), lambda c: (0, 0, c)),
            pl.BlockSpec((2, 512, 512), lambda c: (0, c, 0)),
        ],
        scratch_shapes=[pltpu.VMEM((2, N, 512), F32)],
        compiler_params=pltpu.CompilerParams(vmem_limit_bytes=60 * 2**20),
    )(trail.reshape(2, 8, N, 128), lhs, w, piv)


def shards(piv_cols, trail_cols, row_end, parent_of):
    parent = jnp.broadcast_to(parent_of[:, None], (8, 128))
    trail, lhs, w, piv = main_call(piv_cols, trail_cols, row_end, parent)
    r_trail, r_pivot = solve_trail(trail, lhs, w, piv)
    return r_pivot, r_trail


def solution(mesh):
    return jax.shard_map(
        shards,
        mesh=mesh,
        in_specs=(P("sub", None, "front"), P("sub", None, "front"), P("sub", None), P("sub")),
        out_specs=(P(None, None, "front"), P(None, None, "front")),
        check_vma=False,
    )
```

```python
import jax
import jax.numpy as jnp
from jax import lax
from jax.experimental import pallas as pl
from jax.experimental.pallas import tpu as pltpu
from jax.sharding import PartitionSpec as P

F32 = jnp.float32
BF = jnp.bfloat16
MESH = pl.DeviceIdType.MESH
LIVE = 1280
N = 1024
T = 1024
COLORS = 6
HALVINGS = 4
PIVOT_ROWS = (384,) * 6
TRAIL_ROWS = (1408,) * 4 + (1280,) * 2


def dims_of(sub):
    x, y, z = sub % 4, (sub // 4) % 4, sub // 16
    partner, side = [], []
    for kind in range(2):
        for coord, stride in ((x, 1), (y, 4), (z, 16)):
            if kind == 0:
                other, bit = coord + 1 - 2 * (coord % 2), ((coord + 1) // 2) % 2
            else:
                other, bit = 3 - coord, coord // 2
            partner.append(sub + (other - coord) * stride)
            side.append(bit)
    return partner, side


def rows_at(start, size):
    return pl.ds(pl.multiple_of(start, 8), size)


def step_of(h):
    return h if h <= 96 else max(d for d in range(8, 97, 8) if h % d == 0)


class Exchange:
    def __init__(self, rows, g, work, inbox, total, send, recv, partner, side, weights):
        self.rows, self.g, self.work, self.inbox, self.total = rows, g, work, inbox, total
        self.send, self.recv, self.partner, self.side, self.weights = send, recv, partner, side, weights
        self.off = [sum(rows[:q]) for q in range(COLORS)]
        self.rel = [0] * COLORS
        self.flying = {}

    def size(self, q, s):
        return self.rows[q] >> (min(s, HALVINGS - 1) + 1)

    def describe(self, q, s, slot, src, dst):
        d = (q + s) % 6
        self.flying[q, slot] = pltpu.make_async_remote_copy(
            src, dst, self.send.at[q, slot], self.recv.at[q, slot],
            device_id={"sub": self.partner[d]}, device_id_type=MESH)

    def describe_scatter(self, q, s):
        d, h = (q + s) % 6, self.size(q, s)
        if s == 0:
            src = self.g.at[rows_at(self.off[q] + (1 - self.side[d]) * h, h), :]
            dst = self.inbox[0].at[q, pl.ds(0, h), :]
        else:
            start = self.rel[q] + ((1 - self.side[d]) * h if s < HALVINGS else 0)
            src = self.work.at[q, :, rows_at(start, h), :]
            dst = self.inbox[s].at[q, :, pl.ds(0, h), :]
        self.describe(q, s, s, src, dst)

    def start_piece(self, i):
        for q in range(COLORS):
            h = self.size(q, 0)
            start = self.off[q] + (1 - self.side[q]) * h + i * (h // 4)
            pltpu.make_async_remote_copy(
                self.g.at[rows_at(start, h // 4), :], self.inbox[0].at[q, pl.ds(i * (h // 4), h // 4), :],
                self.send.at[q, 0], self.recv.at[q, 0],
                device_id={"sub": self.partner[q]}, device_id_type=MESH).start()

    def start_scatter(self, q, s):
        self.describe_scatter(q, s)
        self.flying[q, s].start()

    def scatter(self, q, s):
        d, h = (q + s) % 6, self.size(q, s)
        step = step_of(h)
        if s < HALVINGS:
            self.off[q] = self.off[q] + self.side[d] * h
            if s:
                self.rel[q] = self.rel[q] + self.side[d] * h
        off, rel, work, inbox = self.off[q], self.rel[q], self.work, self.inbox[s]
        self.flying[q, s].wait()
        if s == 0:
            weights = self.weights(q)

        @pl.loop(0, h // step)
        def _(i):
            there = rows_at(i * step, step)
            here = rows_at(rel + i * step, step)
            if s == 0:
                mine, theirs = self.g[rows_at(off + i * step, step), :], inbox[q, there, :]
                for p in range(2):
                    work[q, p, there, :] = mine * weights[p][0] + theirs * weights[p][1]
            elif s < 5:
                work[q, :, here, :] = work[q, :, here, :] + inbox[q, :, there, :]
            else:
                self.total[:, rows_at(off + i * step, step), :] = work[q, :, here, :] + inbox[q, :, there, :]

        if s < 5:
            self.start_scatter(q, s + 1)
        else:
            self.start_gather(q, HALVINGS - 1)

    def describe_gather(self, q, s):
        rows = self.total.at[:, rows_at(self.off[q], self.size(q, s)), :]
        self.describe(q, s, 6 + s, rows, rows)

    def start_gather(self, q, s):
        self.describe_gather(q, s)
        self.flying[q, 6 + s].start()

    def gather(self, q, s):
        d, h = (q + s) % 6, self.size(q, s)
        self.flying[q, 6 + s].wait()
        theirs = self.off[q] + (1 - 2 * self.side[d]) * h
        self.off[q] = self.off[q] - self.side[d] * h
        if s > 0:
            self.start_gather(q, s - 1)
        return theirs, h


def split(x):
    h = x.astype(BF)
    r = x - h.astype(F32)
    m = r.astype(BF)
    l = (r - m.astype(F32)).astype(BF)
    return h, m, l


def stack_rhs(x, count):
    h, m, l = split(x)
    return jnp.concatenate([h, m, h, l, m, h][:count], axis=0)


def stack_lhs(h, m, l=None):
    return jnp.concatenate([h, h, m] if l is None else [h, h, m, h, m, l], axis=1)


def dot(a, b):
    return lax.dot_general(a, b, (((1,), (0,)), ((), ())), preferred_element_type=F32)


def spread(x):
    return jnp.broadcast_to(x, (8, 128))


def low_dot(out):
    h = out.astype(BF).astype(F32)
    r = out - h
    m = r.astype(BF).astype(F32)
    l = r - m
    left = jnp.concatenate([h, h, m, h, m, l], axis=0)[:, :128].astype(BF)
    right = jnp.concatenate([h, m, h, l, m, h], axis=0).astype(BF)
    return lax.dot_general(left, right, (((0,), (0,)), ((), ())), preferred_element_type=F32)


def leaf(s, first, last):
    sub = lax.broadcasted_iota(jnp.int32, (8, 256), 0)
    for g in range(first, last):
        for p in range(2):
            rows = [s[p, pl.ds(8 * g + j, 8, stride=0), :] for j in range(8)]
            if g < 15:
                nxt = s[p, 8 * g + 8 : 8 * g + 16, :]
                cols = [spread(nxt[:, 8 * g + j : 8 * g + j + 1]) for j in range(8)]
            a = {(i, j): spread(rows[i][:, 8 * g + j : 8 * g + j + 1]) for i in range(8) for j in range(i, 8)}
            m, u = {}, {}
            for k in range(8):
                r = lax.rsqrt(a[k, k])
                for j in range(k + 1, 8):
                    u[k, j] = a[k, j] * r
                m[k, k] = r
                for c in range(k):
                    m[k, c] = m[k, c] * r
                for i in range(k + 1, 8):
                    for j in range(i, 8):
                        a[i, j] = a[i, j] - u[k, i] * u[k, j]
                    for c in range(k + 1):
                        t = u[k, i] * m[k, c]
                        m[i, c] = (m[i, c] - t) if (i, c) in m else -t
            done = []
            for k in range(8):
                lo = sum(m[k, j] * rows[j][:, :128] for j in range(k + 1))
                hi = sum(m[k, j] * rows[j][:, 128:] for j in range(k + 1))
                done.append(jnp.concatenate([lo, hi], axis=1))
            out = done[0]
            for k in range(1, 8):
                out = jnp.where(sub == k, done[k], out)
            s[p, 8 * g : 8 * g + 8, :] = out
            if g < 15:
                lo, hi = nxt[:, :128], nxt[:, 128:]
                for k in range(8):
                    l = sum(m[k, j] * cols[j] for j in range(k + 1))
                    lo = lo - l * done[k][:, :128]
                    hi = hi - l * done[k][:, 128:]
                s[p, 8 * g + 8 : 8 * g + 16, :] = jnp.concatenate([lo, hi], axis=1)
            if g < 14:
                upd = low_dot(out)
                s[p, 8 * g + 16 :, :] = s[p, 8 * g + 16 :, :] - upd[8 * g + 16 :, :]


def block_of(core, b):
    t, o = 2 * core + b // 9, b % 9
    c = (o + t) // 8
    return t + c * (7 - 2 * t), (1 - c) * (t + o) + c * (o - 1)


def main_kernel(piv, trail, row_end, parent, trail_out, lhs_out, w_out, piv_out,
                half_in, cols_in, turned, gp, wp, totp, pair, gt, wt, ut, u, s, rhs, lhs, low, w,
                p0, p1, p2, p3, p4, p5, t0, t1, t2, t3, t4, t5, pids,
                in_sem, sendp, recvp, sendt, recvt, psend, precv, dsend, drecv, hsend, hrecv, out_sem, lhs_sem, trail_sem):
    front = lax.axis_index("front")
    sub = lax.axis_index("sub")
    partner, side = dims_of(sub)

    local = [pltpu.make_async_copy(piv.at[0, pl.ds(0, LIVE), :], half_in.at[front], in_sem.at[0])]
    for j in range(4):
        local.append(pltpu.make_async_copy(
            trail.at[0, pl.ds(0, LIVE), pl.ds(256 * j, 256)], cols_in.at[j], in_sem.at[1 + j]))
    for copy in local:
        copy.start()

    barrier = pltpu.get_barrier_semaphore()
    for d in range(6):
        pl.semaphore_signal(barrier, inc=1, device_id={"sub": partner[d]}, device_id_type=MESH)
    pl.semaphore_signal(barrier, inc=1, device_id={"front": 1 - front}, device_id_type=MESH)
    pl.semaphore_wait(barrier, 7)

    half = pltpu.make_async_remote_copy(
        piv.at[0, pl.ds(0, LIVE), :], half_in.at[front], hsend, hrecv,
        device_id={"front": 1 - front}, device_id_type=MESH)
    half.start()
    pid_copies = []
    for q in range(COLORS):
        copy = pltpu.make_async_remote_copy(
            parent, pids.at[q], psend.at[q], precv.at[q],
            device_id={"sub": partner[q]}, device_id_type=MESH)
        copy.start()
        pid_copies.append(copy)

    def weights(q):
        own, other = parent[0:1, 0:1], pids[q, 0:1, 0:1]
        return [((own == p).astype(F32), (other == p).astype(F32)) for p in range(2)]

    pivots = Exchange(PIVOT_ROWS, gp, wp, (p0, p1, p2, p3, p4, p5), totp, sendp, recvp, partner, side, weights)
    trails = Exchange(TRAIL_ROWS, gt, wt, (t0, t1, t2, t3, t4, t5), ut, sendt, recvt, partner, side, weights)

    row_ids = lax.broadcasted_iota(jnp.int32, (LIVE, 128), 0)

    def block(i):
        return pl.ds(pl.multiple_of(i * 128, 128), 128)

    def turn(which):
        @pl.loop(0, 4)
        def _(b):
            value = half_in[which, :, block(b)].astype(F32)
            value = jnp.where(row_ids < row_end[0, which * 4 + b], value, 0.0)
            turned[block(which * 4 + b), :] = jnp.transpose(value).astype(BF)

    local[0].wait()
    turn(front)
    half.wait()
    turn(1 - front)

    for strip in range(2):
        t = 2 * front + strip
        left = jnp.concatenate([turned[block(t), :], turned[block(7 - t), :]], axis=0)

        @pl.loop(0, 4)
        def _(c):
            value = dot(left, half_in[c // 2, :, pl.ds(pl.multiple_of((c % 2) * 256, 256), 256)])
            for e in range(2):
                col = 2 * c + e
                upper = (col - t + 8) // 8
                slot = upper * (strip * 9 + col - t) + (1 - upper) * 18
                gp[block(slot), :] = value[:128, 128 * e : 128 * e + 128]
                upper = (col + t + 1) // 8
                slot = upper * (strip * 9 + col + 1) + (1 - upper) * 18
                gp[block(slot), :] = value[128:, 128 * e : 128 * e + 128]

        for q in range(3 * strip, 3 * strip + 3):
            pivots.start_scatter(q, 0)
    for copy in pid_copies:
        copy.wait()

    def trail_gram(j):
        local[1 + j].wait()

        value = dot(turned[...], cols_in[j])
        gt[2 * j * 1024 : (2 * j + 1) * 1024, :] = value[:, :128]
        gt[(2 * j + 1) * 1024 : (2 * j + 2) * 1024, :] = value[:, 128:]

    for st in range(6):
        if st < 2:
            trail_gram(2 * st)
            trail_gram(2 * st + 1)
        for q in range(COLORS):
            pivots.scatter(q, st)
        if st >= 2:
            trails.start_piece(st - 2)

    to_pair = []

    def start_pair(q, k, start, size):
        rows = rows_at(start, size)
        copy = pltpu.make_async_remote_copy(
            totp.at[:, rows, :], pair.at[:, rows, :], dsend.at[q, k], drecv.at[q, k],
            device_id={"front": 1 - front}, device_id_type=MESH)
        copy.start()
        to_pair.append(copy)

    for q in range(COLORS):
        start_pair(q, 4, pivots.off[q], pivots.size(q, 3))
    for st in range(3, -1, -1):
        for q in range(COLORS):
            start, size = pivots.gather(q, st)
            start_pair(q, st, start, size)
        if st == 1:
            for q in range(COLORS):
                trails.describe_scatter(q, 0)
            for q in range(COLORS):
                trails.scatter(q, 0)

    def place(core, src):
        @pl.loop(0, 18)
        def _(b):
            i, j = block_of(core, b)
            for p in range(2):
                u[p, block(i), block(j)] = src[p, block(b), :]

    place(front, totp)
    for copy in to_pair:
        copy.wait()
    place(1 - front, pair)

    def trail_copy(q, part):
        off, h = states[9][0][q], trails.size(q, 0)
        rows = rows_at(off if part == 0 else off + (1 - 2 * side[q]) * h, h)
        return pltpu.make_async_copy(ut.at[:, rows, :], trail_out.at[:, rows, :], trail_sem.at[q, part])

    def tick(n):
        for q in range(COLORS):
            if n < 6:
                trails.scatter(q, n)
            else:
                trails.gather(q, 9 - n)
            if n >= 8:
                trail_copy(q, n - 8).start()

    plan = {1: (0, 3), 2: (1, 2), 3: (1, 5), 4: (2, 3), 5: (3, 0), 6: (3, 4), 7: (4, 3), 8: (5, 5), 9: (7, 5)}

    def ticks(k, place_):
        for n, (kk, where) in plan.items():
            if where == place_:
                yield n, kk

    ri = lax.broadcasted_iota(jnp.int32, (128, 128), 0)
    ci = lax.broadcasted_iota(jnp.int32, (128, 128), 1)

    states = {}
    for n in range(1, 10):
        states[n] = (list(trails.off), list(trails.rel))
        for q in range(COLORS):
            st = n if n < 6 else 9 - n
            d, h = (q + st) % 6, trails.size(q, st)
            if n < HALVINGS:
                trails.off[q] = trails.off[q] + side[d] * h
                if n:
                    trails.rel[q] = trails.rel[q] + side[d] * h
            elif n >= 6:
                trails.off[q] = trails.off[q] - side[d] * h

    def rebuild(n):
        off, rel = states[n]
        trails.off, trails.rel = list(off), list(rel)
        trails.flying = {}
        for q in range(COLORS):
            if n < 6:
                trails.describe_scatter(q, n)
            else:
                trails.describe_gather(q, 9 - n)

    def run_ticks(k, where):
        for n, kk in ticks(k, where):
            @pl.when(k == kk)
            def _():
                rebuild(n)
                tick(n)

    @pl.loop(0, 8)
    def _(k):
        rs = block(k)
        for p in range(2):
            d = u[p, rs, rs]
            s[p, :, :128] = jnp.where(ri <= ci, d, jnp.transpose(d))
            s[p, :, 128:] = (ri == ci).astype(F32)
        for part in range(4):
            leaf(s, 4 * part, 4 * part + 4)
            run_ticks(k, part)
        for p in range(2):
            wh, wm, wl = split(s[p, :, 128:])
            w[p, k] = jnp.concatenate([wh, wm], axis=1)
            wst = stack_lhs(wh, wm, wl)
            for t in range(2):
                cs = pl.ds(t * 512, 512)
                r = dot(wst, stack_rhs(u[p, rs, cs], 6))
                cols = lax.broadcasted_iota(jnp.int32, (128, 512), 1) + t * 512
                r = jnp.where(cols >= (k + 1) * 128, r, 0.0)
                u[p, rs, cs] = r
                rhs[p, :, cs] = stack_rhs(r, 6)
                th, tm, tl = split(jnp.transpose(r))
                lhs[p, k, cs, :] = jnp.concatenate([th, tm], axis=1)
                low[p, cs, :] = tl
            u[p, rs, rs] = jnp.where(ri <= ci, s[p, :, :128], 0.0)
            pltpu.make_async_copy(lhs.at[p, k], lhs_out.at[p, k], lhs_sem.at[p, k]).start()

        run_ticks(k, 4)

        @pl.loop((k + 1) // 2, 4)
        def _(c):
            rows = pl.ds(pl.multiple_of(c * 256, 256), 256)
            for p in range(2):
                l = lhs[p, k, rows, :]
                l = stack_lhs(l[:, :128], l[:, 128:], low[p, rows, :])

                @pl.loop(c, 4)
                def _(j):
                    cols = pl.ds(pl.multiple_of(j * 256, 256), 256)
                    u[p, rows, cols] = u[p, rows, cols] - dot(l, rhs[p, :, cols])

        run_ticks(k, 5)

    own = pl.ds(pl.multiple_of(front * 512, 512), 512)
    last = [pltpu.make_async_copy(w, w_out, out_sem.at[0])]
    last[0].start()
    for q in range(COLORS):
        last += [trail_copy(q, 0), trail_copy(q, 1)]
    for p in range(2):
        copy = pltpu.make_async_copy(u.at[p, :, own], piv_out.at[p], out_sem.at[1 + p])
        copy.start()
        last.append(copy)
        for k in range(8):
            last.append(pltpu.make_async_copy(lhs.at[p, k], lhs_out.at[p, k], lhs_sem.at[p, k]))
    for copy in last:
        copy.wait()


def main_call(piv, trail, row_end, parent):
    dma = pltpu.SemaphoreType.DMA

    def inbox(rows):
        top = max(rows)
        sizes = [top >> (min(s, HALVINGS - 1) + 1) for s in range(6)]
        return [pltpu.VMEM((COLORS, sizes[0], 128), F32)] + [pltpu.VMEM((COLORS, 2, h, 128), F32) for h in sizes[1:]]

    return pl.pallas_call(
        main_kernel,
        out_shape=(
            jax.ShapeDtypeStruct((2, 8 * N, 128), F32),
            jax.ShapeDtypeStruct((2, 8, N, 256), BF),
            jax.ShapeDtypeStruct((2, 8, 128, 256), BF),
            jax.ShapeDtypeStruct((2, N, 512), F32),
        ),
        in_specs=[
            pl.BlockSpec(memory_space=pl.ANY),
            pl.BlockSpec(memory_space=pl.ANY),
            pl.BlockSpec(memory_space=pltpu.SMEM),
            pl.BlockSpec(memory_space=pltpu.VMEM),
        ],
        out_specs=[pl.BlockSpec(memory_space=pl.ANY)] * 4,
        scratch_shapes=[
            pltpu.VMEM((2, LIVE, 512), BF),
            pltpu.VMEM((4, LIVE, 256), BF),
            pltpu.VMEM((N, LIVE), BF),
            pltpu.VMEM((2304 + 128, 128), F32),
            pltpu.VMEM((COLORS, 2, 192, 128), F32),
            pltpu.VMEM((2, 2304, 128), F32),
            pltpu.VMEM((2, 2304, 128), F32),
            pltpu.VMEM((8 * N, 128), F32),
            pltpu.VMEM((COLORS, 2, 704, 128), F32),
            pltpu.VMEM((2, 8 * N, 128), F32),
            pltpu.VMEM((2, N, N), F32),
            pltpu.VMEM((2, 128, 256), F32),
            pltpu.VMEM((2, 768, N), BF),
            pltpu.VMEM((2, 8, N, 256), BF),
            pltpu.VMEM((2, N, 128), BF),
            pltpu.VMEM((2, 8, 128, 256), BF),
            *inbox(PIVOT_ROWS),
            *inbox(TRAIL_ROWS),
            pltpu.VMEM((COLORS, 8, 128), jnp.int32),
            dma((5,)),
            dma((COLORS, 10)),
            dma((COLORS, 10)),
            dma((COLORS, 10)),
            dma((COLORS, 10)),
            dma((COLORS,)),
            dma((COLORS,)),
            dma((COLORS, 5)),
            dma((COLORS, 5)),
            dma,
            dma,
            dma((3,)),
            dma((2, 8)),
            dma((COLORS, 2)),
        ],
        compiler_params=pltpu.CompilerParams(
            collective_id=0, has_side_effects=True, vmem_limit_bytes=67043328),
    )(piv, trail, row_end, parent)


def solve_kernel(trail, lhs_in, w, piv, r_trail, r_piv, v, lhs, sem):
    fetch = [pltpu.make_async_copy(lhs_in.at[:, k], lhs.at[:, k], sem.at[k]) for k in range(8)]

    @pl.when(pl.program_id(0) == 0)
    def _():
        for copy in fetch:
            copy.start()

    r_piv[...] = piv[...]
    for p in range(2):
        for j in range(4):
            v[p, :, 128 * j : 128 * j + 128] = trail[p, j]

    for k in range(8):
        rows = slice(128 * k, 128 * k + 128)
        rest = slice(128 * k + 128, N)
        right = []
        for p in range(2):
            wk = w[p, k]
            r = dot(stack_lhs(wk[:, :128], wk[:, 128:]), stack_rhs(v[p, rows, :], 3))
            r_trail[p, rows, :] = r
            right.append(stack_rhs(r, 3))
        if k == 7:
            break

        @pl.when(pl.program_id(0) == 0)
        def _():
            fetch[k].wait()

        for p in range(2):
            l = lhs[p, k, rest, :]
            v[p, rest, :] = v[p, rest, :] - dot(stack_lhs(l[:, :128], l[:, 128:]), right[p])

    @pl.when(pl.program_id(0) == 0)
    def _():
        fetch[7].wait()


def solve_trail(trail, lhs, w, piv):
    whole = pl.Buffered(1)
    return pl.pallas_call(
        solve_kernel,
        grid=(2,),
        out_shape=(jax.ShapeDtypeStruct((2, N, T), F32), jax.ShapeDtypeStruct((2, N, 512), F32)),
        in_specs=[
            pl.BlockSpec((2, 4, N, 128), lambda c: (0, c, 0, 0)),
            pl.BlockSpec(memory_space=pl.ANY),
            pl.BlockSpec((2, 8, 128, 256), lambda c: (0, 0, 0, 0), pipeline_mode=whole),
            pl.BlockSpec((2, 512, 512), lambda c: (0, c, 0)),
        ],
        out_specs=[
            pl.BlockSpec((2, N, 512), lambda c: (0, 0, c)),
            pl.BlockSpec((2, 512, 512), lambda c: (0, c, 0)),
        ],
        scratch_shapes=[pltpu.VMEM((2, N, 512), F32), pltpu.VMEM((2, 8, N, 256), BF), pltpu.SemaphoreType.DMA((8,))],
        compiler_params=pltpu.CompilerParams(vmem_limit_bytes=60 * 2**20),
    )(trail.reshape(2, 8, N, 128), lhs, w, piv)


def shards(piv_cols, trail_cols, row_end, parent_of):
    parent = jnp.broadcast_to(parent_of[:, None], (8, 128))
    trail, lhs, w, piv = main_call(piv_cols, trail_cols, row_end, parent)
    r_trail, r_pivot = solve_trail(trail, lhs, w, piv)
    return r_pivot, r_trail


def solution(mesh):
    return jax.shard_map(
        shards,
        mesh=mesh,
        in_specs=(P("sub", None, "front"), P("sub", None, "front"), P("sub", None), P("sub")),
        out_specs=(P(None, None, "front"), P(None, None, "front")),
        check_vma=False,
    )
```

```python
import jax
import jax.numpy as jnp
from jax import lax
from jax.experimental import pallas as pl
from jax.experimental.pallas import tpu as pltpu
from jax.sharding import PartitionSpec as P

F32 = jnp.float32
BF = jnp.bfloat16
MESH = pl.DeviceIdType.MESH
LIVE = 1280
N = 1024
T = 1024
COLORS = 6
HALVINGS = 4
PIVOT_ROWS = (384,) * 6
PLAN = ((2, 7, 9, 11, 14, 17, 20, 25, 36), (5, 8, 10, 13, 16, 18, 22, 29, 43))
TRAIL_ROWS = ((768,) * 2 + (640,) * 4, (640,) * 4 + (768,) * 2)


def dims_of(sub):
    x, y, z = sub % 4, (sub // 4) % 4, sub // 16
    partner, side = [], []
    for kind in range(2):
        for coord, stride in ((x, 1), (y, 4), (z, 16)):
            if kind == 0:
                other, bit = coord + 1 - 2 * (coord % 2), ((coord + 1) // 2) % 2
            else:
                other, bit = 3 - coord, coord // 2
            partner.append(sub + (other - coord) * stride)
            side.append(bit)
    return partner, side


def rows_at(start, size):
    return pl.ds(pl.multiple_of(start, 8), size)


def step_of(h):
    return h if h <= 96 else max(d for d in range(8, 97, 8) if h % d == 0)


class Exchange:
    def __init__(self, rows, g, work, inbox, total, send, recv, partner, side, weights, first=0):
        self.rows, self.g, self.work, self.inbox, self.total = rows, g, work, inbox, total
        self.send, self.recv, self.partner, self.side, self.weights = send, recv, partner, side, weights
        self.off = [first + sum(rows[:q]) for q in range(COLORS)]
        self.rel = [0] * COLORS
        self.flying = {}

    def size(self, q, s):
        return self.rows[q] >> (min(s, HALVINGS - 1) + 1)

    def describe(self, q, s, slot, src, dst):
        d = (q + s) % 6
        self.flying[q, slot] = pltpu.make_async_remote_copy(
            src, dst, self.send.at[q, slot], self.recv.at[q, slot],
            device_id={"sub": self.partner[d]}, device_id_type=MESH)

    def describe_scatter(self, q, s):
        d, h = (q + s) % 6, self.size(q, s)
        if s == 0:
            src = self.g.at[rows_at(self.off[q] + (1 - self.side[d]) * h, h), :]
            dst = self.inbox[0].at[q, pl.ds(0, h), :]
        else:
            start = self.rel[q] + ((1 - self.side[d]) * h if s < HALVINGS else 0)
            src = self.work.at[q, :, rows_at(start, h), :]
            dst = self.inbox[s].at[q, :, pl.ds(0, h), :]
        self.describe(q, s, s, src, dst)

    def start_piece(self, i):
        for q in range(COLORS):
            h = self.size(q, 0)
            start = self.off[q] + (1 - self.side[q]) * h + i * (h // 2)
            pltpu.make_async_remote_copy(
                self.g.at[rows_at(start, h // 2), :], self.inbox[0].at[q, pl.ds(i * (h // 2), h // 2), :],
                self.send.at[q, 0], self.recv.at[q, 0],
                device_id={"sub": self.partner[q]}, device_id_type=MESH).start()

    def start_scatter(self, q, s):
        self.describe_scatter(q, s)
        self.flying[q, s].start()

    def scatter(self, q, s):
        d, h = (q + s) % 6, self.size(q, s)
        step = step_of(h)
        if s < HALVINGS:
            self.off[q] = self.off[q] + self.side[d] * h
            if s:
                self.rel[q] = self.rel[q] + self.side[d] * h
        off, rel, work, inbox = self.off[q], self.rel[q], self.work, self.inbox[s]
        self.flying[q, s].wait()
        if s == 0:
            weights = self.weights(q)

        @pl.loop(0, h // step)
        def _(i):
            there = rows_at(i * step, step)
            here = rows_at(rel + i * step, step)
            if s == 0:
                mine, theirs = self.g[rows_at(off + i * step, step), :], inbox[q, there, :]
                for p in range(2):
                    work[q, p, there, :] = mine * weights[p][0] + theirs * weights[p][1]
            elif s < 5:
                work[q, :, here, :] = work[q, :, here, :] + inbox[q, :, there, :]
            else:
                self.total[:, rows_at(off + i * step, step), :] = work[q, :, here, :] + inbox[q, :, there, :]

        if s < 5:
            self.start_scatter(q, s + 1)
        else:
            self.start_gather(q, HALVINGS - 1)

    def describe_gather(self, q, s):
        rows = self.total.at[:, rows_at(self.off[q], self.size(q, s)), :]
        self.describe(q, s, 6 + s, rows, rows)

    def start_gather(self, q, s):
        self.describe_gather(q, s)
        self.flying[q, 6 + s].start()

    def gather(self, q, s):
        d, h = (q + s) % 6, self.size(q, s)
        self.flying[q, 6 + s].wait()
        theirs = self.off[q] + (1 - 2 * self.side[d]) * h
        self.off[q] = self.off[q] - self.side[d] * h
        if s > 0:
            self.start_gather(q, s - 1)
        return theirs, h


def split(x):
    h = x.astype(BF)
    return h, (x - h.astype(F32)).astype(BF)


def stack_rhs(x):
    h, m = split(x)
    return jnp.concatenate([h, m, h], axis=0)


def stack_lhs(h, m):
    return jnp.concatenate([h, h, m], axis=1)


def dot(a, b):
    return lax.dot_general(a, b, (((1,), (0,)), ((), ())), preferred_element_type=F32)


def spread(x):
    return jnp.broadcast_to(x, (8, 128))


def low_dot(out):
    h = out.astype(BF).astype(F32)
    r = out - h
    m = r.astype(BF).astype(F32)
    l = r - m
    left = jnp.concatenate([h, h, m, h, m, l], axis=0)[:, :128].astype(BF)
    right = jnp.concatenate([h, m, h, l, m, h], axis=0).astype(BF)
    return lax.dot_general(left, right, (((0,), (0,)), ((), ())), preferred_element_type=F32)


def leaf(s, first, last):
    sub = lax.broadcasted_iota(jnp.int32, (8, 256), 0)
    for g in range(first, last):
        for p in range(2):
            rows = [s[p, pl.ds(8 * g + j, 8, stride=0), :] for j in range(8)]
            if g < 15:
                nxt = s[p, 8 * g + 8 : 8 * g + 16, :]
                cols = [spread(nxt[:, 8 * g + j : 8 * g + j + 1]) for j in range(8)]
            a = {(i, j): spread(rows[i][:, 8 * g + j : 8 * g + j + 1]) for i in range(8) for j in range(i, 8)}
            m, u = {}, {}
            for k in range(8):
                r = lax.rsqrt(a[k, k])
                for j in range(k + 1, 8):
                    u[k, j] = a[k, j] * r
                m[k, k] = r
                for c in range(k):
                    m[k, c] = m[k, c] * r
                for i in range(k + 1, 8):
                    for j in range(i, 8):
                        a[i, j] = a[i, j] - u[k, i] * u[k, j]
                    for c in range(k + 1):
                        t = u[k, i] * m[k, c]
                        m[i, c] = (m[i, c] - t) if (i, c) in m else -t
            done = []
            for k in range(8):
                lo = sum(m[k, j] * rows[j][:, :128] for j in range(k + 1))
                hi = sum(m[k, j] * rows[j][:, 128:] for j in range(k + 1))
                done.append(jnp.concatenate([lo, hi], axis=1))
            out = done[0]
            for k in range(1, 8):
                out = jnp.where(sub == k, done[k], out)
            s[p, 8 * g : 8 * g + 8, :] = out
            if g < 15:
                lo, hi = nxt[:, :128], nxt[:, 128:]
                for k in range(8):
                    l = sum(m[k, j] * cols[j] for j in range(k + 1))
                    lo = lo - l * done[k][:, :128]
                    hi = hi - l * done[k][:, 128:]
                s[p, 8 * g + 8 : 8 * g + 16, :] = jnp.concatenate([lo, hi], axis=1)
            if g < 14:
                upd = low_dot(out)
                s[p, 8 * g + 16 :, :] = s[p, 8 * g + 16 :, :] - upd[8 * g + 16 :, :]


def block_of(core, b):
    t, o = 2 * core + b // 9, b % 9
    c = (o + t) // 8
    return t + c * (7 - 2 * t), (1 - c) * (t + o) + c * (o - 1)


def main_kernel(piv, trail, row_end, parent, trail_out, lhs_out, w_out, piv_out,
                half_in, cols_in, turned, gp, wp, totp, pair, gt, wt, wt2, ut, u, s, rhs, lhs, w,
                p0, p1, p2, p3, p4, p5, t0, t1, t2, t3, t4, t5, y0, y1, y2, y3, y4, y5, pids,
                in_sem, sendp, recvp, sendt, recvt, sendy, recvy, psend, precv, dsend, drecv, hsend, hrecv, out_sem, lhs_sem, trail_sem):
    front = lax.axis_index("front")
    sub = lax.axis_index("sub")
    partner, side = dims_of(sub)

    local = [pltpu.make_async_copy(piv.at[0, pl.ds(0, LIVE), :], half_in.at[front], in_sem.at[0])]
    for j in range(4):
        local.append(pltpu.make_async_copy(
            trail.at[0, pl.ds(0, LIVE), pl.ds(256 * j, 256)], cols_in.at[j], in_sem.at[1 + j]))
    for copy in local:
        copy.start()

    barrier = pltpu.get_barrier_semaphore()
    for d in range(6):
        pl.semaphore_signal(barrier, inc=1, device_id={"sub": partner[d]}, device_id_type=MESH)
    pl.semaphore_signal(barrier, inc=1, device_id={"front": 1 - front}, device_id_type=MESH)
    pl.semaphore_wait(barrier, 7)

    half = pltpu.make_async_remote_copy(
        piv.at[0, pl.ds(0, LIVE), :], half_in.at[front], hsend, hrecv,
        device_id={"front": 1 - front}, device_id_type=MESH)
    half.start()
    pid_copies = []
    for q in range(COLORS):
        copy = pltpu.make_async_remote_copy(
            parent, pids.at[q], psend.at[q], precv.at[q],
            device_id={"sub": partner[q]}, device_id_type=MESH)
        copy.start()
        pid_copies.append(copy)

    def weights(q):
        own, other = parent[0:1, 0:1], pids[q, 0:1, 0:1]
        return [((own == p).astype(F32), (other == p).astype(F32)) for p in range(2)]

    pivots = Exchange(PIVOT_ROWS, gp, wp, (p0, p1, p2, p3, p4, p5), totp, sendp, recvp, partner, side, weights)
    trails = (
        Exchange(TRAIL_ROWS[0], gt, wt, (t0, t1, t2, t3, t4, t5), ut, sendt, recvt, partner, side, weights),
        Exchange(TRAIL_ROWS[1], gt, wt2, (y0, y1, y2, y3, y4, y5), ut, sendy, recvy, partner, side, weights, 4 * N),
    )

    row_ids = lax.broadcasted_iota(jnp.int32, (LIVE, 128), 0)

    def block(i):
        return pl.ds(pl.multiple_of(i * 128, 128), 128)

    def turn(which):
        @pl.loop(0, 4)
        def _(b):
            value = half_in[which, :, block(b)].astype(F32)
            value = jnp.where(row_ids < row_end[0, which * 4 + b], value, 0.0)
            turned[block(which * 4 + b), :] = jnp.transpose(value).astype(BF)

    local[0].wait()
    turn(front)
    half.wait()
    turn(1 - front)

    for strip in range(2):
        t = 2 * front + strip
        left = jnp.concatenate([turned[block(t), :], turned[block(7 - t), :]], axis=0)

        @pl.loop(0, 4)
        def _(c):
            value = dot(left, half_in[c // 2, :, pl.ds(pl.multiple_of((c % 2) * 256, 256), 256)])
            for e in range(2):
                col = 2 * c + e
                upper = (col - t + 8) // 8
                slot = upper * (strip * 9 + col - t) + (1 - upper) * 18
                gp[block(slot), :] = value[:128, 128 * e : 128 * e + 128]
                upper = (col + t + 1) // 8
                slot = upper * (strip * 9 + col + 1) + (1 - upper) * 18
                gp[block(slot), :] = value[128:, 128 * e : 128 * e + 128]

        for q in range(3 * strip, 3 * strip + 3):
            pivots.start_scatter(q, 0)
    for copy in pid_copies:
        copy.wait()

    def trail_gram(j):
        local[1 + j].wait()

        value = dot(turned[...], cols_in[j])
        gt[2 * j * 1024 : (2 * j + 1) * 1024, :] = value[:, :128]
        gt[(2 * j + 1) * 1024 : (2 * j + 2) * 1024, :] = value[:, 128:]

    for st in range(6):
        if st < 2:
            trail_gram(2 * st)
            trail_gram(2 * st + 1)
        for q in range(COLORS):
            pivots.scatter(q, st)
        if st >= 2:
            trails[(st - 2) // 2].start_piece(st % 2)

    to_pair = []

    def start_pair(q, k, start, size):
        rows = rows_at(start, size)
        copy = pltpu.make_async_remote_copy(
            totp.at[:, rows, :], pair.at[:, rows, :], dsend.at[q, k], drecv.at[q, k],
            device_id={"front": 1 - front}, device_id_type=MESH)
        copy.start()
        to_pair.append(copy)

    for q in range(COLORS):
        start_pair(q, 4, pivots.off[q], pivots.size(q, 3))
    for st in range(3, -1, -1):
        for q in range(COLORS):
            start, size = pivots.gather(q, st)
            start_pair(q, st, start, size)
        if st == 1:
            for part in trails:
                for q in range(COLORS):
                    part.describe_scatter(q, 0)
                for q in range(COLORS):
                    part.scatter(q, 0)

    def place(core, src):
        @pl.loop(0, 18)
        def _(b):
            i, j = block_of(core, b)
            for p in range(2):
                u[p, block(i), block(j)] = src[p, block(b), :]

    place(front, totp)
    for copy in to_pair:
        copy.wait()
    place(1 - front, pair)

    def trail_copy(x, q, part):
        off, h = states[x, 9][0][q], trails[x].size(q, 0)
        rows = rows_at(off if part == 0 else off + (1 - 2 * side[q]) * h, h)
        return pltpu.make_async_copy(ut.at[:, rows, :], trail_out.at[:, rows, :], trail_sem.at[x, q, part])

    def tick(x, n):
        for q in range(COLORS):
            if n < 6:
                trails[x].scatter(q, n)
            else:
                trails[x].gather(q, 9 - n)
            if n >= 8:
                trail_copy(x, q, n - 8).start()

    plan = {}
    for x in range(2):
        for n in range(1, 10):
            plan[x, n] = (PLAN[x][n - 1] // 6, PLAN[x][n - 1] % 6)

    def ticks(k, place_):
        for key, (kk, where) in sorted(plan.items(), key=lambda e: (e[0][1], e[0][0])):
            if where == place_:
                yield key, kk

    ri = lax.broadcasted_iota(jnp.int32, (128, 128), 0)
    ci = lax.broadcasted_iota(jnp.int32, (128, 128), 1)

    states = {}
    for x, part in enumerate(trails):
        for n in range(1, 10):
            states[x, n] = (list(part.off), list(part.rel))
            for q in range(COLORS):
                st = n if n < 6 else 9 - n
                d, h = (q + st) % 6, part.size(q, st)
                if n < HALVINGS:
                    part.off[q] = part.off[q] + side[d] * h
                    part.rel[q] = part.rel[q] + side[d] * h
                elif n >= 6:
                    part.off[q] = part.off[q] - side[d] * h

    def rebuild(x, n):
        part = trails[x]
        part.off, part.rel = list(states[x, n][0]), list(states[x, n][1])
        part.flying = {}
        for q in range(COLORS):
            if n < 6:
                part.describe_scatter(q, n)
            else:
                part.describe_gather(q, 9 - n)

    def run_ticks(k, where):
        for (x, n), kk in ticks(k, where):
            @pl.when(k == kk)
            def _():
                rebuild(x, n)
                tick(x, n)

    @pl.loop(0, 8)
    def _(k):
        rs = block(k)
        for p in range(2):
            d = u[p, rs, rs]
            s[p, :, :128] = jnp.where(ri <= ci, d, jnp.transpose(d))
            s[p, :, 128:] = (ri == ci).astype(F32)
        for part in range(4):
            leaf(s, 4 * part, 4 * part + 4)
            run_ticks(k, part)
        for p in range(2):
            wh, wm = split(s[p, :, 128:])
            w[p, k] = jnp.concatenate([wh, wm], axis=1)
            wst = stack_lhs(wh, wm)
            for t in range(2):
                cs = pl.ds(t * 512, 512)
                r = dot(wst, stack_rhs(u[p, rs, cs]))
                cols = lax.broadcasted_iota(jnp.int32, (128, 512), 1) + t * 512
                r = jnp.where(cols >= (k + 1) * 128, r, 0.0)
                u[p, rs, cs] = r
                rhs[p, :, cs] = stack_rhs(r)
                th, tm = split(jnp.transpose(r))
                lhs[p, k, cs, :] = jnp.concatenate([th, tm], axis=1)
            u[p, rs, rs] = jnp.where(ri <= ci, s[p, :, :128], 0.0)
            pltpu.make_async_copy(lhs.at[p, k], lhs_out.at[p, k], lhs_sem.at[p, k]).start()

        run_ticks(k, 4)

        @pl.loop((k + 1) // 2, 4)
        def _(c):
            rows = pl.ds(pl.multiple_of(c * 256, 256), 256)
            for p in range(2):
                l = lhs[p, k, rows, :]
                l = stack_lhs(l[:, :128], l[:, 128:])

                @pl.loop(c, 4)
                def _(j):
                    cols = pl.ds(pl.multiple_of(j * 256, 256), 256)
                    u[p, rows, cols] = u[p, rows, cols] - dot(l, rhs[p, :, cols])

        run_ticks(k, 5)

    own = pl.ds(pl.multiple_of(front * 512, 512), 512)
    last = [pltpu.make_async_copy(w, w_out, out_sem.at[0])]
    last[0].start()
    for q in range(COLORS):
        last += [trail_copy(x, q, part) for x in range(2) for part in range(2)]
    for p in range(2):
        copy = pltpu.make_async_copy(u.at[p, :, own], piv_out.at[p], out_sem.at[1 + p])
        copy.start()
        last.append(copy)
        for k in range(8):
            last.append(pltpu.make_async_copy(lhs.at[p, k], lhs_out.at[p, k], lhs_sem.at[p, k]))
    for copy in last:
        copy.wait()


def main_call(piv, trail, row_end, parent):
    dma = pltpu.SemaphoreType.DMA

    def inbox(rows):
        top = max(rows)
        sizes = [top >> (min(s, HALVINGS - 1) + 1) for s in range(6)]
        return [pltpu.VMEM((COLORS, sizes[0], 128), F32)] + [pltpu.VMEM((COLORS, 2, h, 128), F32) for h in sizes[1:]]

    return pl.pallas_call(
        main_kernel,
        out_shape=(
            jax.ShapeDtypeStruct((2, 8 * N, 128), F32),
            jax.ShapeDtypeStruct((2, 8, N, 256), BF),
            jax.ShapeDtypeStruct((2, 8, 128, 256), BF),
            jax.ShapeDtypeStruct((2, N, 512), F32),
        ),
        in_specs=[
            pl.BlockSpec(memory_space=pl.ANY),
            pl.BlockSpec(memory_space=pl.ANY),
            pl.BlockSpec(memory_space=pltpu.SMEM),
            pl.BlockSpec(memory_space=pltpu.VMEM),
        ],
        out_specs=[pl.BlockSpec(memory_space=pl.ANY)] * 4,
        scratch_shapes=[
            pltpu.VMEM((2, LIVE, 512), BF),
            pltpu.VMEM((4, LIVE, 256), BF),
            pltpu.VMEM((N, LIVE), BF),
            pltpu.VMEM((2304 + 128, 128), F32),
            pltpu.VMEM((COLORS, 2, 192, 128), F32),
            pltpu.VMEM((2, 2304, 128), F32),
            pltpu.VMEM((2, 2304, 128), F32),
            pltpu.VMEM((8 * N, 128), F32),
            pltpu.VMEM((COLORS, 2, 384, 128), F32),
            pltpu.VMEM((COLORS, 2, 384, 128), F32),
            pltpu.VMEM((2, 8 * N, 128), F32),
            pltpu.VMEM((2, N, N), F32),
            pltpu.VMEM((2, 128, 256), F32),
            pltpu.VMEM((2, 384, N), BF),
            pltpu.VMEM((2, 8, N, 256), BF),
            pltpu.VMEM((2, 8, 128, 256), BF),
            *inbox(PIVOT_ROWS),
            *inbox(TRAIL_ROWS[0]),
            *inbox(TRAIL_ROWS[1]),
            pltpu.VMEM((COLORS, 8, 128), jnp.int32),
            dma((5,)),
            dma((COLORS, 10)),
            dma((COLORS, 10)),
            dma((COLORS, 10)),
            dma((COLORS, 10)),
            dma((COLORS, 10)),
            dma((COLORS, 10)),
            dma((COLORS,)),
            dma((COLORS,)),
            dma((COLORS, 5)),
            dma((COLORS, 5)),
            dma,
            dma,
            dma((3,)),
            dma((2, 8)),
            dma((2, COLORS, 2)),
        ],
        compiler_params=pltpu.CompilerParams(
            collective_id=0, has_side_effects=True, vmem_limit_bytes=67043328),
    )(piv, trail, row_end, parent)


def solve_kernel(trail, lhs_in, w, piv, r_trail, r_piv, v, lhs, sem):
    fetch = [pltpu.make_async_copy(lhs_in.at[:, k], lhs.at[:, k], sem.at[k]) for k in range(8)]

    @pl.when(pl.program_id(0) == 0)
    def _():
        for copy in fetch:
            copy.start()

    r_piv[...] = piv[...]
    for p in range(2):
        for j in range(4):
            v[p, :, 128 * j : 128 * j + 128] = trail[p, j]

    for k in range(8):
        rows = slice(128 * k, 128 * k + 128)
        rest = slice(128 * k + 128, N)
        right = []
        for p in range(2):
            wk = w[p, k]
            r = dot(stack_lhs(wk[:, :128], wk[:, 128:]), stack_rhs(v[p, rows, :]))
            r_trail[p, rows, :] = r
            right.append(stack_rhs(r))
        if k == 7:
            break

        @pl.when(pl.program_id(0) == 0)
        def _():
            fetch[k].wait()

        for p in range(2):
            l = lhs[p, k, rest, :]
            v[p, rest, :] = v[p, rest, :] - dot(stack_lhs(l[:, :128], l[:, 128:]), right[p])

    @pl.when(pl.program_id(0) == 0)
    def _():
        fetch[7].wait()


def solve_trail(trail, lhs, w, piv):
    whole = pl.Buffered(1)
    return pl.pallas_call(
        solve_kernel,
        grid=(2,),
        out_shape=(jax.ShapeDtypeStruct((2, N, T), F32), jax.ShapeDtypeStruct((2, N, 512), F32)),
        in_specs=[
            pl.BlockSpec((2, 4, N, 128), lambda c: (0, c, 0, 0)),
            pl.BlockSpec(memory_space=pl.ANY),
            pl.BlockSpec((2, 8, 128, 256), lambda c: (0, 0, 0, 0), pipeline_mode=whole),
            pl.BlockSpec((2, 512, 512), lambda c: (0, c, 0)),
        ],
        out_specs=[
            pl.BlockSpec((2, N, 512), lambda c: (0, 0, c)),
            pl.BlockSpec((2, 512, 512), lambda c: (0, c, 0)),
        ],
        scratch_shapes=[pltpu.VMEM((2, N, 512), F32), pltpu.VMEM((2, 8, N, 256), BF), pltpu.SemaphoreType.DMA((8,))],
        compiler_params=pltpu.CompilerParams(vmem_limit_bytes=60 * 2**20),
    )(trail.reshape(2, 8, N, 128), lhs, w, piv)


def shards(piv_cols, trail_cols, row_end, parent_of):
    parent = jnp.broadcast_to(parent_of[:, None], (8, 128))
    trail, lhs, w, piv = main_call(piv_cols, trail_cols, row_end, parent)
    r_trail, r_pivot = solve_trail(trail, lhs, w, piv)
    return r_pivot, r_trail


def solution(mesh):
    return jax.shard_map(
        shards,
        mesh=mesh,
        in_specs=(P("sub", None, "front"), P("sub", None, "front"), P("sub", None), P("sub")),
        out_specs=(P(None, None, "front"), P(None, None, "front")),
        check_vma=False,
    )
```

```python
import jax
import jax.numpy as jnp
from jax import lax
from jax.experimental import pallas as pl
from jax.experimental.pallas import tpu as pltpu
from jax.sharding import PartitionSpec as P

F32 = jnp.float32
BF = jnp.bfloat16
MESH = pl.DeviceIdType.MESH
LIVE = 1280
N = 1024
T = 1024
COLORS = 6
HALVINGS = 4
PIVOT_ROWS = (384,) * 6
PLAN = ((2, 7, 9, 11, 14, 17, 20, 25, 36), (5, 8, 10, 13, 16, 18, 22, 29, 43))
TRAIL_ROWS = ((768,) * 2 + (640,) * 4, (640,) * 4 + (768,) * 2)


def dims_of(sub):
    x, y, z = sub % 4, (sub // 4) % 4, sub // 16
    partner, side = [], []
    for kind in range(2):
        for coord, stride in ((x, 1), (y, 4), (z, 16)):
            if kind == 0:
                other, bit = coord + 1 - 2 * (coord % 2), ((coord + 1) // 2) % 2
            else:
                other, bit = 3 - coord, coord // 2
            partner.append(sub + (other - coord) * stride)
            side.append(bit)
    return partner, side


def rows_at(start, size):
    return pl.ds(pl.multiple_of(start, 8), size)


def step_of(h):
    return h if h <= 96 else max(d for d in range(8, 97, 8) if h % d == 0)


class Exchange:
    def __init__(self, rows, g, work, inbox, total, send, recv, partner, side, weights, first=0):
        self.rows, self.g, self.work, self.inbox, self.total = rows, g, work, inbox, total
        self.send, self.recv, self.partner, self.side, self.weights = send, recv, partner, side, weights
        self.off = [first + sum(rows[:q]) for q in range(COLORS)]
        self.rel = [0] * COLORS
        self.flying = {}

    def size(self, q, s):
        return self.rows[q] >> (min(s, HALVINGS - 1) + 1)

    def describe(self, q, s, slot, src, dst):
        d = (q + s) % 6
        self.flying[q, slot] = pltpu.make_async_remote_copy(
            src, dst, self.send.at[q, slot], self.recv.at[q, slot],
            device_id={"sub": self.partner[d]}, device_id_type=MESH)

    def describe_scatter(self, q, s):
        d, h = (q + s) % 6, self.size(q, s)
        if s == 0:
            src = self.g.at[rows_at(self.off[q] + (1 - self.side[d]) * h, h), :]
            dst = self.inbox[0].at[q, pl.ds(0, h), :]
        else:
            start = self.rel[q] + ((1 - self.side[d]) * h if s < HALVINGS else 0)
            src = self.work.at[q, :, rows_at(start, h), :]
            dst = self.inbox[s].at[q, :, pl.ds(0, h), :]
        self.describe(q, s, s, src, dst)

    def start_piece(self, i):
        for q in range(COLORS):
            h = self.size(q, 0)
            start = self.off[q] + (1 - self.side[q]) * h + i * (h // 2)
            pltpu.make_async_remote_copy(
                self.g.at[rows_at(start, h // 2), :], self.inbox[0].at[q, pl.ds(i * (h // 2), h // 2), :],
                self.send.at[q, 0], self.recv.at[q, 0],
                device_id={"sub": self.partner[q]}, device_id_type=MESH).start()

    def start_scatter(self, q, s):
        self.describe_scatter(q, s)
        self.flying[q, s].start()

    def scatter(self, q, s):
        d, h = (q + s) % 6, self.size(q, s)
        step = step_of(h)
        if s < HALVINGS:
            self.off[q] = self.off[q] + self.side[d] * h
            if s:
                self.rel[q] = self.rel[q] + self.side[d] * h
        off, rel, work, inbox = self.off[q], self.rel[q], self.work, self.inbox[s]
        self.flying[q, s].wait()
        if s == 0:
            weights = self.weights(q)

        @pl.loop(0, h // step)
        def _(i):
            there = rows_at(i * step, step)
            here = rows_at(rel + i * step, step)
            if s == 0:
                mine, theirs = self.g[rows_at(off + i * step, step), :], inbox[q, there, :]
                for p in range(2):
                    work[q, p, there, :] = mine * weights[p][0] + theirs * weights[p][1]
            elif s < 5:
                work[q, :, here, :] = work[q, :, here, :] + inbox[q, :, there, :]
            else:
                self.total[:, rows_at(off + i * step, step), :] = work[q, :, here, :] + inbox[q, :, there, :]

        if s < 5:
            self.start_scatter(q, s + 1)
        else:
            self.start_gather(q, HALVINGS - 1)

    def describe_gather(self, q, s):
        rows = self.total.at[:, rows_at(self.off[q], self.size(q, s)), :]
        self.describe(q, s, 6 + s, rows, rows)

    def start_gather(self, q, s):
        self.describe_gather(q, s)
        self.flying[q, 6 + s].start()

    def gather(self, q, s):
        d, h = (q + s) % 6, self.size(q, s)
        self.flying[q, 6 + s].wait()
        theirs = self.off[q] + (1 - 2 * self.side[d]) * h
        self.off[q] = self.off[q] - self.side[d] * h
        if s > 0:
            self.start_gather(q, s - 1)
        return theirs, h


def split(x):
    h = x.astype(BF)
    return h, (x - h.astype(F32)).astype(BF)


def stack_rhs(x):
    h, m = split(x)
    return jnp.concatenate([h, m, h], axis=0)


def stack_lhs(h, m):
    return jnp.concatenate([h, h, m], axis=1)


def dot(a, b):
    return lax.dot_general(a, b, (((1,), (0,)), ((), ())), preferred_element_type=F32)


def spread(x):
    return jnp.broadcast_to(x, (8, 128))


def low_dot(out):
    h = out.astype(BF).astype(F32)
    r = out - h
    m = r.astype(BF).astype(F32)
    l = r - m
    left = jnp.concatenate([h, h, m, h, m, l], axis=0)[:, :128].astype(BF)
    right = jnp.concatenate([h, m, h, l, m, h], axis=0).astype(BF)
    return lax.dot_general(left, right, (((0,), (0,)), ((), ())), preferred_element_type=F32)


def tree(terms):
    while len(terms) > 1:
        terms = [a + b for a, b in zip(terms[::2], terms[1::2])] + terms[len(terms) // 2 * 2 :]
    return terms[0]


def leaf(s, first, last):
    sub = lax.broadcasted_iota(jnp.int32, (8, 256), 0)
    for g in range(first, last):
        for p in range(2):
            rows = [s[p, pl.ds(8 * g + j, 8, stride=0), :] for j in range(8)]
            if g < 15:
                nxt = s[p, 8 * g + 8 : 8 * g + 16, :]
                cols = [spread(nxt[:, 8 * g + j : 8 * g + j + 1]) for j in range(8)]
            a = {(i, j): spread(rows[i][:, 8 * g + j : 8 * g + j + 1]) for i in range(8) for j in range(i, 8)}
            m, u = {}, {}
            for k in range(8):
                r = lax.rsqrt(a[k, k])
                for j in range(k + 1, 8):
                    u[k, j] = a[k, j] * r
                m[k, k] = r
                for c in range(k):
                    m[k, c] = m[k, c] * r
                for i in range(k + 1, 8):
                    for j in range(i, 8):
                        a[i, j] = a[i, j] - u[k, i] * u[k, j]
                    for c in range(k + 1):
                        t = u[k, i] * m[k, c]
                        m[i, c] = (m[i, c] - t) if (i, c) in m else -t
            done = []
            for k in range(8):
                lo = tree([m[k, j] * rows[j][:, :128] for j in range(k + 1)])
                hi = tree([m[k, j] * rows[j][:, 128:] for j in range(k + 1)])
                done.append(jnp.concatenate([lo, hi], axis=1))
            out = done[0]
            for k in range(1, 8):
                out = jnp.where(sub == k, done[k], out)
            s[p, 8 * g : 8 * g + 8, :] = out
            if g < 15:
                lo, hi = nxt[:, :128], nxt[:, 128:]
                for k in range(8):
                    l = tree([m[k, j] * cols[j] for j in range(k + 1)])
                    lo = lo - l * done[k][:, :128]
                    hi = hi - l * done[k][:, 128:]
                s[p, 8 * g + 8 : 8 * g + 16, :] = jnp.concatenate([lo, hi], axis=1)
            if g < 14:
                upd = low_dot(out)
                s[p, 8 * g + 16 :, :] = s[p, 8 * g + 16 :, :] - upd[8 * g + 16 :, :]


def block_of(core, b):
    t, o = 2 * core + b // 9, b % 9
    c = (o + t) // 8
    return t + c * (7 - 2 * t), (1 - c) * (t + o) + c * (o - 1)


def main_kernel(piv, trail, row_end, parent, trail_out, lhs_out, w_out, piv_out,
                half_in, cols_in, turned, gp, wp, totp, pair, gt, wt, wt2, ut, u, s, rhs, lhs, w,
                p0, p1, p2, p3, p4, p5, t0, t1, t2, t3, t4, t5, y0, y1, y2, y3, y4, y5, pids,
                in_sem, sendp, recvp, sendt, recvt, sendy, recvy, psend, precv, dsend, drecv, hsend, hrecv, out_sem, lhs_sem, trail_sem):
    front = lax.axis_index("front")
    sub = lax.axis_index("sub")
    partner, side = dims_of(sub)

    local = [pltpu.make_async_copy(piv.at[0, pl.ds(0, LIVE), :], half_in.at[front], in_sem.at[0])]
    for j in range(4):
        local.append(pltpu.make_async_copy(
            trail.at[0, pl.ds(0, LIVE), pl.ds(256 * j, 256)], cols_in.at[j], in_sem.at[1 + j]))
    for copy in local:
        copy.start()

    barrier = pltpu.get_barrier_semaphore()
    for d in range(6):
        pl.semaphore_signal(barrier, inc=1, device_id={"sub": partner[d]}, device_id_type=MESH)
    pl.semaphore_signal(barrier, inc=1, device_id={"front": 1 - front}, device_id_type=MESH)
    pl.semaphore_wait(barrier, 7)

    half = pltpu.make_async_remote_copy(
        piv.at[0, pl.ds(0, LIVE), :], half_in.at[front], hsend, hrecv,
        device_id={"front": 1 - front}, device_id_type=MESH)
    half.start()
    pid_copies = []
    for q in range(COLORS):
        copy = pltpu.make_async_remote_copy(
            parent, pids.at[q], psend.at[q], precv.at[q],
            device_id={"sub": partner[q]}, device_id_type=MESH)
        copy.start()
        pid_copies.append(copy)

    def weights(q):
        own, other = parent[0:1, 0:1], pids[q, 0:1, 0:1]
        return [((own == p).astype(F32), (other == p).astype(F32)) for p in range(2)]

    pivots = Exchange(PIVOT_ROWS, gp, wp, (p0, p1, p2, p3, p4, p5), totp, sendp, recvp, partner, side, weights)
    trails = (
        Exchange(TRAIL_ROWS[0], gt, wt, (t0, t1, t2, t3, t4, t5), ut, sendt, recvt, partner, side, weights),
        Exchange(TRAIL_ROWS[1], gt, wt2, (y0, y1, y2, y3, y4, y5), ut, sendy, recvy, partner, side, weights, 4 * N),
    )

    row_ids = lax.broadcasted_iota(jnp.int32, (LIVE, 128), 0)

    def block(i):
        return pl.ds(pl.multiple_of(i * 128, 128), 128)

    def turn(which):
        @pl.loop(0, 4)
        def _(b):
            value = half_in[which, :, block(b)].astype(F32)
            value = jnp.where(row_ids < row_end[0, which * 4 + b], value, 0.0)
            turned[block(which * 4 + b), :] = jnp.transpose(value).astype(BF)

    local[0].wait()
    turn(front)
    half.wait()
    turn(1 - front)

    for strip in range(2):
        t = 2 * front + strip
        left = jnp.concatenate([turned[block(t), :], turned[block(7 - t), :]], axis=0)

        @pl.loop(0, 4)
        def _(c):
            value = dot(left, half_in[c // 2, :, pl.ds(pl.multiple_of((c % 2) * 256, 256), 256)])
            for e in range(2):
                col = 2 * c + e
                upper = (col - t + 8) // 8
                slot = upper * (strip * 9 + col - t) + (1 - upper) * 18
                gp[block(slot), :] = value[:128, 128 * e : 128 * e + 128]
                upper = (col + t + 1) // 8
                slot = upper * (strip * 9 + col + 1) + (1 - upper) * 18
                gp[block(slot), :] = value[128:, 128 * e : 128 * e + 128]

        for q in range(3 * strip, 3 * strip + 3):
            pivots.start_scatter(q, 0)
    for copy in pid_copies:
        copy.wait()

    def trail_gram(j):
        local[1 + j].wait()

        value = dot(turned[...], cols_in[j])
        gt[2 * j * 1024 : (2 * j + 1) * 1024, :] = value[:, :128]
        gt[(2 * j + 1) * 1024 : (2 * j + 2) * 1024, :] = value[:, 128:]

    for st in range(6):
        if st < 2:
            trail_gram(2 * st)
            trail_gram(2 * st + 1)
        for q in range(COLORS):
            pivots.scatter(q, st)
        if st >= 2:
            trails[(st - 2) // 2].start_piece(st % 2)

    to_pair = []

    def start_pair(q, k, start, size):
        rows = rows_at(start, size)
        copy = pltpu.make_async_remote_copy(
            totp.at[:, rows, :], pair.at[:, rows, :], dsend.at[q, k], drecv.at[q, k],
            device_id={"front": 1 - front}, device_id_type=MESH)
        copy.start()
        to_pair.append(copy)

    for q in range(COLORS):
        start_pair(q, 4, pivots.off[q], pivots.size(q, 3))
    for st in range(3, -1, -1):
        for q in range(COLORS):
            start, size = pivots.gather(q, st)
            start_pair(q, st, start, size)
        if st == 1:
            for part in trails:
                for q in range(COLORS):
                    part.describe_scatter(q, 0)
                for q in range(COLORS):
                    part.scatter(q, 0)

    def place(core, src):
        @pl.loop(0, 18)
        def _(b):
            i, j = block_of(core, b)
            for p in range(2):
                u[p, block(i), block(j)] = src[p, block(b), :]

    place(front, totp)
    for copy in to_pair:
        copy.wait()
    place(1 - front, pair)

    def trail_copy(x, q, part):
        off, h = states[x, 9][0][q], trails[x].size(q, 0)
        rows = rows_at(off if part == 0 else off + (1 - 2 * side[q]) * h, h)
        return pltpu.make_async_copy(ut.at[:, rows, :], trail_out.at[:, rows, :], trail_sem.at[x, q, part])

    def tick(x, n):
        for q in range(COLORS):
            if n < 6:
                trails[x].scatter(q, n)
            else:
                trails[x].gather(q, 9 - n)
            if n >= 8:
                trail_copy(x, q, n - 8).start()

    plan = {}
    for x in range(2):
        for n in range(1, 10):
            plan[x, n] = (PLAN[x][n - 1] // 6, PLAN[x][n - 1] % 6)

    def ticks(k, place_):
        for key, (kk, where) in sorted(plan.items(), key=lambda e: (e[0][1], e[0][0])):
            if where == place_:
                yield key, kk

    ri = lax.broadcasted_iota(jnp.int32, (128, 128), 0)
    ci = lax.broadcasted_iota(jnp.int32, (128, 128), 1)

    states = {}
    for x, part in enumerate(trails):
        for n in range(1, 10):
            states[x, n] = (list(part.off), list(part.rel))
            for q in range(COLORS):
                st = n if n < 6 else 9 - n
                d, h = (q + st) % 6, part.size(q, st)
                if n < HALVINGS:
                    part.off[q] = part.off[q] + side[d] * h
                    part.rel[q] = part.rel[q] + side[d] * h
                elif n >= 6:
                    part.off[q] = part.off[q] - side[d] * h

    def rebuild(x, n):
        part = trails[x]
        part.off, part.rel = list(states[x, n][0]), list(states[x, n][1])
        part.flying = {}
        for q in range(COLORS):
            if n < 6:
                part.describe_scatter(q, n)
            else:
                part.describe_gather(q, 9 - n)

    def run_ticks(k, where):
        for (x, n), kk in ticks(k, where):
            @pl.when(k == kk)
            def _():
                rebuild(x, n)
                tick(x, n)

    @pl.loop(0, 8)
    def _(k):
        rs = block(k)
        for p in range(2):
            d = u[p, rs, rs]
            s[p, :, :128] = jnp.where(ri <= ci, d, jnp.transpose(d))
            s[p, :, 128:] = (ri == ci).astype(F32)
        for part in range(4):
            leaf(s, 4 * part, 4 * part + 4)
            run_ticks(k, part)
        for p in range(2):
            wh, wm = split(s[p, :, 128:])
            w[p, k] = jnp.concatenate([wh, wm], axis=1)
            wst = stack_lhs(wh, wm)
            for t in range(2):
                cs = pl.ds(t * 512, 512)
                r = dot(wst, stack_rhs(u[p, rs, cs]))
                cols = lax.broadcasted_iota(jnp.int32, (128, 512), 1) + t * 512
                r = jnp.where(cols >= (k + 1) * 128, r, 0.0)
                u[p, rs, cs] = r
                rhs[p, :, cs] = stack_rhs(r)
                th, tm = split(jnp.transpose(r))
                lhs[p, k, cs, :] = jnp.concatenate([th, tm], axis=1)
            u[p, rs, rs] = jnp.where(ri <= ci, s[p, :, :128], 0.0)
            pltpu.make_async_copy(lhs.at[p, k], lhs_out.at[p, k], lhs_sem.at[p, k]).start()

        run_ticks(k, 4)

        @pl.loop((k + 1) // 2, 4)
        def _(c):
            rows = pl.ds(pl.multiple_of(c * 256, 256), 256)
            for p in range(2):
                l = lhs[p, k, rows, :]
                l = stack_lhs(l[:, :128], l[:, 128:])

                @pl.loop(c, 4)
                def _(j):
                    cols = pl.ds(pl.multiple_of(j * 256, 256), 256)
                    u[p, rows, cols] = u[p, rows, cols] - dot(l, rhs[p, :, cols])

        run_ticks(k, 5)

    own = pl.ds(pl.multiple_of(front * 512, 512), 512)
    last = [pltpu.make_async_copy(w, w_out, out_sem.at[0])]
    last[0].start()
    for q in range(COLORS):
        last += [trail_copy(x, q, part) for x in range(2) for part in range(2)]
    for p in range(2):
        copy = pltpu.make_async_copy(u.at[p, :, own], piv_out.at[p], out_sem.at[1 + p])
        copy.start()
        last.append(copy)
        for k in range(8):
            last.append(pltpu.make_async_copy(lhs.at[p, k], lhs_out.at[p, k], lhs_sem.at[p, k]))
    for copy in last:
        copy.wait()


def main_call(piv, trail, row_end, parent):
    dma = pltpu.SemaphoreType.DMA

    def inbox(rows):
        top = max(rows)
        sizes = [top >> (min(s, HALVINGS - 1) + 1) for s in range(6)]
        return [pltpu.VMEM((COLORS, sizes[0], 128), F32)] + [pltpu.VMEM((COLORS, 2, h, 128), F32) for h in sizes[1:]]

    return pl.pallas_call(
        main_kernel,
        out_shape=(
            jax.ShapeDtypeStruct((2, 8 * N, 128), F32),
            jax.ShapeDtypeStruct((2, 8, N, 256), BF),
            jax.ShapeDtypeStruct((2, 8, 128, 256), BF),
            jax.ShapeDtypeStruct((2, N, 512), F32),
        ),
        in_specs=[
            pl.BlockSpec(memory_space=pl.ANY),
            pl.BlockSpec(memory_space=pl.ANY),
            pl.BlockSpec(memory_space=pltpu.SMEM),
            pl.BlockSpec(memory_space=pltpu.VMEM),
        ],
        out_specs=[pl.BlockSpec(memory_space=pl.ANY)] * 4,
        scratch_shapes=[
            pltpu.VMEM((2, LIVE, 512), BF),
            pltpu.VMEM((4, LIVE, 256), BF),
            pltpu.VMEM((N, LIVE), BF),
            pltpu.VMEM((2304 + 128, 128), F32),
            pltpu.VMEM((COLORS, 2, 192, 128), F32),
            pltpu.VMEM((2, 2304, 128), F32),
            pltpu.VMEM((2, 2304, 128), F32),
            pltpu.VMEM((8 * N, 128), F32),
            pltpu.VMEM((COLORS, 2, 384, 128), F32),
            pltpu.VMEM((COLORS, 2, 384, 128), F32),
            pltpu.VMEM((2, 8 * N, 128), F32),
            pltpu.VMEM((2, N, N), F32),
            pltpu.VMEM((2, 128, 256), F32),
            pltpu.VMEM((2, 384, N), BF),
            pltpu.VMEM((2, 8, N, 256), BF),
            pltpu.VMEM((2, 8, 128, 256), BF),
            *inbox(PIVOT_ROWS),
            *inbox(TRAIL_ROWS[0]),
            *inbox(TRAIL_ROWS[1]),
            pltpu.VMEM((COLORS, 8, 128), jnp.int32),
            dma((5,)),
            dma((COLORS, 10)),
            dma((COLORS, 10)),
            dma((COLORS, 10)),
            dma((COLORS, 10)),
            dma((COLORS, 10)),
            dma((COLORS, 10)),
            dma((COLORS,)),
            dma((COLORS,)),
            dma((COLORS, 5)),
            dma((COLORS, 5)),
            dma,
            dma,
            dma((3,)),
            dma((2, 8)),
            dma((2, COLORS, 2)),
        ],
        compiler_params=pltpu.CompilerParams(
            collective_id=0, has_side_effects=True, vmem_limit_bytes=67043328),
    )(piv, trail, row_end, parent)


def solve_kernel(trail, lhs_in, w, piv, r_trail, r_piv, v, lhs, sem):
    fetch = [pltpu.make_async_copy(lhs_in.at[:, k], lhs.at[:, k], sem.at[k]) for k in range(8)]

    @pl.when(pl.program_id(0) == 0)
    def _():
        for copy in fetch:
            copy.start()

    r_piv[...] = piv[...]
    for p in range(2):
        for j in range(4):
            v[p, :, 128 * j : 128 * j + 128] = trail[p, j]

    for k in range(8):
        rows = slice(128 * k, 128 * k + 128)
        rest = slice(128 * k + 128, N)
        right = []
        for p in range(2):
            wk = w[p, k]
            r = dot(stack_lhs(wk[:, :128], wk[:, 128:]), stack_rhs(v[p, rows, :]))
            r_trail[p, rows, :] = r
            right.append(stack_rhs(r))
        if k == 7:
            break

        @pl.when(pl.program_id(0) == 0)
        def _():
            fetch[k].wait()

        for p in range(2):
            l = lhs[p, k, rest, :]
            v[p, rest, :] = v[p, rest, :] - dot(stack_lhs(l[:, :128], l[:, 128:]), right[p])

    @pl.when(pl.program_id(0) == 0)
    def _():
        fetch[7].wait()


def solve_trail(trail, lhs, w, piv):
    whole = pl.Buffered(1)
    return pl.pallas_call(
        solve_kernel,
        grid=(2,),
        out_shape=(jax.ShapeDtypeStruct((2, N, T), F32), jax.ShapeDtypeStruct((2, N, 512), F32)),
        in_specs=[
            pl.BlockSpec((2, 4, N, 128), lambda c: (0, c, 0, 0)),
            pl.BlockSpec(memory_space=pl.ANY),
            pl.BlockSpec((2, 8, 128, 256), lambda c: (0, 0, 0, 0), pipeline_mode=whole),
            pl.BlockSpec((2, 512, 512), lambda c: (0, c, 0)),
        ],
        out_specs=[
            pl.BlockSpec((2, N, 512), lambda c: (0, 0, c)),
            pl.BlockSpec((2, 512, 512), lambda c: (0, c, 0)),
        ],
        scratch_shapes=[pltpu.VMEM((2, N, 512), F32), pltpu.VMEM((2, 8, N, 256), BF), pltpu.SemaphoreType.DMA((8,))],
        compiler_params=pltpu.CompilerParams(vmem_limit_bytes=60 * 2**20),
    )(trail.reshape(2, 8, N, 128), lhs, w, piv)


def shards(piv_cols, trail_cols, row_end, parent_of):
    parent = jnp.broadcast_to(parent_of[:, None], (8, 128))
    trail, lhs, w, piv = main_call(piv_cols, trail_cols, row_end, parent)
    r_trail, r_pivot = solve_trail(trail, lhs, w, piv)
    return r_pivot, r_trail


def solution(mesh):
    return jax.shard_map(
        shards,
        mesh=mesh,
        in_specs=(P("sub", None, "front"), P("sub", None, "front"), P("sub", None), P("sub")),
        out_specs=(P(None, None, "front"), P(None, None, "front")),
        check_vma=False,
    )
```
